32 devices in a mesh: trade: 4 (over y, core), scen: 8 (over z, x).
Axes of the slice: x: 2, y: 2, z: 4, core: 2. Of those that a mesh axis runs over, the one named last changes fastest.
Arguments:
- factors: float32 [2048, 64], P('scen'), may hold values from -1 to 1
- feat_factor: int32 [1024], replicated, may hold values from 0 to 63
- feat_degree: int32 [1024], replicated, may hold values from 1 to 12
- coefficients: float32 [1024, 8192], P(None, 'trade'), may hold values from -0.1875 to 0.1875
- set_of_trade: int32 [8192], P('trade'), may hold values from 0 to 511, as said below
- party_of_set: int32 [512], P('trade'), may hold values from 0 to 511
- threshold: float32 [512], replicated, may hold values from 0 to 4
- weight: float32 [512], replicated, may hold values from 0.5 to 2
Outputs:
- xva: float32 [512], P('trade')
- coef_sens: float32 [1024, 8192], P('scen', 'trade')
- feature_sens: float32 [1024, 2048], P('trade', 'scen')
The draws below stay inside these ranges and needn't reach their ends.
Inputs may be any that keep to these rules, and one draw needn't show every extreme that they name: `set_of_trade`: each netting set holds exactly 16 trades; the trades of aligned block b of 2048 trades belong to sets b * 128 to (b + 1) * 128 - 1.
All inputs are finite; a program needn't handle non-finite values.
Results may differ from the reference program's by a relative error of at most 0.000073.
Values sent between devices are 32-bit elements; how exact they have to be, the bound alone decides.
No kernel may reach another device: no remote copies, remote signals or barrier semaphores. Data moves between devices by JAX's collectives and lax.ppermute only.
A program may use at most 64 MiB of HBM per device.

```python
import math
import jax
import jax.numpy as jnp
import numpy as np
from jax import lax

K = 1024
NFAC = 64
MAXDEG = 12
SET_SIZE = 16
TR_DEV = 2048
TRADES = 8192
SCEN = 2048
NSETS = 512
NCP = 512


def draw_set_of_trade(key, part):
    blocks = TRADES // TR_DEV
    keys = jax.random.split(jax.random.fold_in(key, 11), blocks)
    orders = jax.vmap(lambda single: jax.random.permutation(single, TR_DEV))(keys)
    offsets = jnp.arange(blocks, dtype=jnp.int32) * (TR_DEV // SET_SIZE)
    sets = orders.astype(jnp.int32) // SET_SIZE + offsets[:, None]
    return sets.reshape(TRADES).astype(jnp.int32)


def with_ends(values, own_key, low, high):
    spot = [jax.random.randint(jax.random.fold_in(own_key, axis), (), 0, length) for axis, length in enumerate(values.shape)]
    widest = values.shape.index(max(values.shape))
    next_to = spot[:widest] + [(spot[widest] + 1) % values.shape[widest]] + spot[widest + 1:]
    return values.at[tuple(spot)].set(low).at[tuple(next_to)].set(high)


def steps_of(key, dims, shards, smallest, high):
    level, own = 1.0, jax.random.fold_in(key, 6)
    for position, blocks in shards:
        draws = jnp.exp(jax.random.uniform(jax.random.fold_in(own, position), (blocks,), jnp.float32, smallest / len(shards), high / len(shards)))
        level = level * jnp.repeat(draws, dims[position] // blocks).reshape([-1 if axis == position else 1 for axis in range(len(dims))])
    return level


def rank_table(number_of, slope):
    portions = [(1 << 20) // math.isqrt(standing ** slope) + 1 for standing in range(1, number_of + 1)]
    scale = 1 + sum(portions) // (1 << 30)
    return np.cumsum(np.array([max(1, weight // scale) for weight in portions]))


def ranked_ids(own_key, dims, count, slope):
    grid = rank_table(count, slope)
    ticket = jax.random.randint(jax.random.fold_in(own_key, 1), dims, 0, int(grid[count - 1]))
    grade = jnp.searchsorted(jnp.asarray(grid, jnp.int32), ticket, side="right")
    return jax.random.permutation(jax.random.fold_in(own_key, 2), count)[grade].astype(jnp.int32)


def scatter_about(stream_key, dims, deviation, reach, shards=(), kind=jnp.bfloat16):
    array = jax.random.normal(stream_key, dims, jnp.float32) * deviation
    if len(shards) > 0:
        array = steps_of(stream_key, dims, shards, -0.22, 0.18) * array
    return jnp.clip(array, min=-reach, max=reach).astype(kind)


def setup_inputs(seed: int = 0) -> dict:
    key_of = jax.random.split(jax.random.key(seed), 9)
    return {
        "factors": jnp.clip(jax.random.uniform(key_of[0], (SCEN, NFAC), jnp.float32, -1.0, 1.0) * steps_of(key_of[0], (SCEN, NFAC), ((0, 8),), -0.4, 0.0), -1.0, 1.0),
        "feat_factor": with_ends(jax.random.randint(key_of[1], (K,), 0, NFAC), jax.random.fold_in(key_of[1], 1), 0, NFAC - 1).astype(jnp.int32),
        "feat_degree": with_ends(jax.random.randint(key_of[2], (K,), 1, MAXDEG + 1), jax.random.fold_in(key_of[2], 1), 1, MAXDEG).astype(jnp.int32),
        "coefficients": scatter_about(key_of[3], (K, TRADES), K ** -0.5, 0.1875, ((1, 4),), jnp.float32),
        "set_of_trade": draw_set_of_trade(jax.random.fold_in(key_of[8], 71), 0),
        "party_of_set": with_ends(ranked_ids(key_of[5], (NSETS,), NCP, 2), jax.random.fold_in(key_of[5], 3), 0, NCP - 1).astype(jnp.int32),
        "threshold": jnp.clip(jax.random.uniform(key_of[6], (NCP,), jnp.float32, 0.0, 4.0), 0.0, 4.0),
        "weight": jnp.clip(jnp.exp(jax.random.uniform(key_of[7], (NCP,), jnp.float32, math.log(0.5), math.log(2.0))), 0.5, 2.0),
    }


highest = lax.Precision.HIGHEST


def chebyshev(points, degrees):
    before = jnp.ones_like(points)
    current = points
    result = jnp.where(degrees[None, :] == 1, current, jnp.zeros_like(points))
    for order in range(2, MAXDEG + 1):
        before, current = current, 2.0 * points * current - before
        result = jnp.where(degrees[None, :] == order, current, result)
    return result


def reference(factors, feat_factor, feat_degree, coefficients, set_of_trade, party_of_set, threshold, weight):
    points = factors[:, feat_factor]
    phi = chebyshev(points, feat_degree)
    folded = jax.ops.segment_sum(coefficients.T, set_of_trade, NSETS).T
    exposure = jnp.dot(phi, folded, precision=highest)
    netted = jax.ops.segment_sum(exposure.T, party_of_set, NCP).T
    shifted = netted - threshold[None, :]
    xva = weight * jnp.sum(jax.nn.softplus(shifted), axis=0) / SCEN
    party_adj = weight[None, :] * jax.nn.sigmoid(shifted)
    set_adj = party_adj[:, party_of_set]
    set_grad = jnp.dot(phi.T, set_adj, precision=highest) / SCEN
    coef_sens = set_grad[:, set_of_trade]
    feature_sens = jnp.dot(folded, set_adj.T, precision=highest)
    return xva, coef_sens, feature_sens
```

```python
import functools

import jax
import jax.numpy as jnp
from jax import lax
from jax.experimental import pallas as pl
from jax.experimental.pallas import tpu as pltpu
from jax.sharding import PartitionSpec as P

MAXDEG = 12
SET_SIZE = 16
INFO = 8

f32 = jnp.float32
bf16 = jnp.bfloat16
VMEM = pl.BlockSpec(memory_space=pltpu.VMEM)
ANY = pl.BlockSpec(memory_space=pl.ANY)


def split(value):
    high = value.astype(bf16)
    low = (value - high.astype(f32)).astype(bf16)
    return high, low


def nn(left, right):
    return lax.dot_general(left, right, (((1,), (0,)), ((), ())), preferred_element_type=f32)


def nt(left, right):
    return lax.dot_general(left, right, (((1,), (1,)), ((), ())), preferred_element_type=f32)


def iota(shape, dim):
    return lax.broadcasted_iota(jnp.int32, shape, dim)


def column(row):
    n = row.shape[1]
    return jnp.transpose(jnp.broadcast_to(row.astype(f32), (n, n)))


def one_hot(test):
    return jnp.where(test, jnp.float32(1), jnp.float32(0)).astype(bf16)


def pick(table, ids, rows):
    lanes = table.shape[1]
    total = jnp.zeros((1, ids.shape[1]), f32)
    for r in range(rows):
        here = column(table[r : r + 1, :])
        where = iota((lanes, ids.shape[1]), 0) + r * lanes == ids
        total = total + jnp.sum(jnp.where(where, here[:, : ids.shape[1]], 0.0), axis=0, keepdims=True)
    return total


def first_kernel(n_trade, fact_ref, factor_ref, degree_ref, coef_hbm, set_ref, party_ref, thr_ref, wgt_ref, *rest):
    folded_refs = rest[:n_trade]
    expo_ref, high_ref, low_ref, coef_buf, sems = rest[n_trade:]
    me = lax.axis_index("trade")
    width, cols = coef_hbm.shape
    sets = cols // SET_SIZE
    nfac, scen = fact_ref.shape
    block = 128
    own = width // n_trade
    steps = width // block
    per = own // block

    def start_row(step):
        return pl.multiple_of((me ^ (step // per)) * own + (step % per) * block, block)

    def copy(step):
        return pltpu.make_async_copy(
            coef_hbm.at[pl.ds(start_row(step), block), :], coef_buf.at[step], sems.at[step]
        )

    for step in range(steps):
        copy(step).start()
    points = fact_ref[...]
    before, current = jnp.ones_like(points), points
    high, low = [], []
    for order in range(1, MAXDEG + 1):
        if order > 1:
            before, current = current, 2.0 * points * current - before
        a, b = split(current)
        high.append(a)
        low.append(b)
    high = jnp.concatenate(high, axis=0)
    low = jnp.concatenate(low, axis=0)
    member = one_hot(set_ref[...] - me * sets == iota((sets, cols), 0))
    party = party_ref[...]
    rows = thr_ref.shape[0]
    thr_row = pick(thr_ref[...], party, rows)
    wgt_row = pick(wgt_ref[...], party, rows)
    info = jnp.where(
        iota((INFO, sets), 0) == 0,
        party.astype(f32),
        jnp.where(iota((INFO, sets), 0) == 1, thr_row, wgt_row),
    )
    expo_ref[sets:, :] = jnp.zeros((INFO, scen), f32)
    expo_ref[sets:, :sets] = info
    exposure = jnp.zeros((sets, scen), f32)
    for step in range(steps):
        row = start_row(step)
        line = lax.div(row, block)
        key = factor_ref[pl.ds(line, 1), :] + nfac * (degree_ref[pl.ds(line, 1), :] - 1)
        key = column(key)
        key = jnp.concatenate([key] * (MAXDEG * nfac // block), axis=1).astype(jnp.int32)
        chosen = one_hot(key == iota(key.shape, 1))
        phi_high = nn(chosen, high).astype(bf16)
        phi_low = nn(chosen, low).astype(bf16)
        high_ref[pl.ds(row, block), :] = phi_high
        low_ref[pl.ds(row, block), :] = phi_low
        copy(step).wait()
        coef_high, coef_low = split(coef_buf[step])
        folded = nt(coef_high, member) + nt(coef_low, member)
        folded_refs[step // per][pl.ds((step % per) * block, block), :] = folded
        turned_high, turned_low = split(jnp.transpose(folded))
        exposure = exposure + nn(turned_high, phi_high) + nn(turned_low, phi_high) + nn(turned_high, phi_low)
    expo_ref[:sets, :] = exposure


def second_kernel(n_trade, n_scen, all_ref, high_ref, low_ref, thr_ref, wgt_ref, adj_ref, *chunk_refs):
    trade, scen = lax.axis_index("trade"), lax.axis_index("scen")
    stride = all_ref.shape[0] // n_trade
    sets = stride - INFO
    chunk = high_ref.shape[0] // n_scen
    infos = [all_ref[a * stride + sets : (a + 1) * stride, :sets] for a in range(n_trade)]
    party_row = jnp.concatenate([info[0:1, :] for info in infos], axis=1).astype(jnp.int32)
    expo = [split(all_ref[a * stride : a * stride + sets, :]) for a in range(n_trade)]
    expo_high = jnp.concatenate([e[0] for e in expo], axis=0)
    expo_low = jnp.concatenate([e[1] for e in expo], axis=0)
    total = party_row.shape[1]
    for a in range(n_trade):
        turned = jnp.transpose(infos[a])
        same = one_hot(turned[:, 0:1].astype(jnp.int32) == party_row)
        netted = nn(same, expo_high) + nn(same, expo_low)
        adj_ref[a * sets : (a + 1) * sets, :] = turned[:, 2:3] * jax.nn.sigmoid(netted - turned[:, 1:2])
    own = one_hot(iota((sets, total), 0) + trade * sets == party_row)
    netted = nn(own, expo_high) + nn(own, expo_low)
    thr_own = column(thr_ref[pl.ds(trade, 1), :])
    soft = jax.nn.softplus(netted - thr_own[:, 0:1])
    summed = jnp.sum(soft, axis=1, keepdims=True)
    xva = jnp.transpose(jnp.broadcast_to(summed, (sets, sets)))[0:INFO, :] * wgt_ref[pl.ds(trade, 1), :]
    mine = adj_ref[pl.ds(pl.multiple_of(trade * sets, sets), sets), :]
    adj_high, adj_low = split(mine)
    for k in range(n_scen):
        rows = pl.ds(pl.multiple_of((scen ^ k) * chunk, chunk), chunk)
        phi_high, phi_low = high_ref[rows, :], low_ref[rows, :]
        part = nt(phi_high, adj_high) + nt(phi_high, adj_low) + nt(phi_low, adj_high)
        chunk_refs[k][:chunk, :] = part
        chunk_refs[k][chunk:, :] = xva


def feature_kernel(n_trade, adj_ref, *refs):
    folded_refs, out_ref = refs[:n_trade], refs[n_trade]
    trade = lax.axis_index("trade")
    sets = folded_refs[0].shape[1]
    total = jnp.zeros(out_ref.shape, f32)
    for k in range(n_trade):
        adj_high, adj_low = split(adj_ref[pl.ds(pl.multiple_of((trade ^ k) * sets, sets), sets), :])
        high, low = split(folded_refs[k][...])
        total = total + nn(high, adj_high) + nn(low, adj_high) + nn(high, adj_low)
    out_ref[...] = total


def last_kernel(n_scen, scale, set_ref, *refs):
    chunk_refs, xva_ref, out_ref = refs[:n_scen], refs[n_scen], refs[n_scen + 1]
    trade = lax.axis_index("trade")
    rows, cols = out_ref.shape
    sets = cols // SET_SIZE
    member = one_hot(set_ref[...] - trade * sets == iota((sets, cols), 0))
    total = chunk_refs[0][...]
    for k in range(1, n_scen):
        total = total + chunk_refs[k][...]
    total = total * scale
    xva_ref[...] = total[rows : rows + 1, :]
    high, low = split(total[:rows, :])
    out_ref[...] = nn(high, member) + nn(low, member)


def call(kernel, out_shape, in_specs, scratch=(), flops=10**9, moved=10**6, name=None):
    return pl.pallas_call(
        kernel,
        out_shape=out_shape,
        in_specs=in_specs,
        out_specs=jax.tree.map(lambda _: VMEM, out_shape),
        scratch_shapes=scratch,
        cost_estimate=pl.CostEstimate(flops=flops, bytes_accessed=moved, transcendentals=0),
        name=name,
    )


def local(
    factors, feat_factor, feat_degree, coefficients, set_of_trade, party_of_set, threshold, weight
):
    n_trade, n_scen = lax.axis_size("trade"), lax.axis_size("scen")
    scen, nfac = factors.shape
    width, cols = coefficients.shape
    sets = cols // SET_SIZE
    lanes = threshold.shape[0] // n_trade
    struct = jax.ShapeDtypeStruct
    thr = threshold.reshape(n_trade, lanes)
    wgt = weight.reshape(n_trade, lanes)
    set_row = set_of_trade.reshape(1, cols)
    own = width // n_trade
    outs = call(
        functools.partial(first_kernel, n_trade),
        [struct((own, sets), f32)] * n_trade
        + [struct((sets + INFO, scen), f32), struct((width, scen), bf16), struct((width, scen), bf16)],
        [VMEM, VMEM, VMEM, ANY, VMEM, VMEM, VMEM, VMEM],
        [pltpu.VMEM((width // 128, 128, cols), f32), pltpu.SemaphoreType.DMA((width // 128,))],
        name="first",
    )(
        factors.T,
        feat_factor.reshape(width // 128, 128),
        feat_degree.reshape(width // 128, 128),
        coefficients,
        set_row,
        party_of_set.reshape(1, sets),
        thr,
        wgt,
    )
    folded, (expo, high, low) = outs[:n_trade], outs[n_trade:]
    everything = lax.all_gather(expo, "trade", axis=0, tiled=True)
    chunk = width // n_scen
    outs = call(
        functools.partial(second_kernel, n_trade, n_scen),
        [struct((n_trade * sets, scen), f32)] + [struct((chunk + INFO, sets), f32)] * n_scen,
        [VMEM] * 5,
        name="second",
    )(everything, high, low, thr, wgt)
    adj, chunks = outs[0], outs[1:]
    chunks = [chunks[0]] + [
        lax.ppermute(chunks[k], "scen", [(i, i ^ k) for i in range(n_scen)]) for k in range(1, n_scen)
    ]
    others = lax.optimization_barrier((adj, *folded[1:]))
    adj, later = others[0], others[1:]
    folded = [folded[0]] + [
        lax.ppermute(later[k - 1], "trade", [(i, i ^ k) for i in range(n_trade)])
        for k in range(1, n_trade)
    ]
    feature_sens = call(
        functools.partial(feature_kernel, n_trade), struct((own, scen), f32), [VMEM] * (n_trade + 1),
        name="feature",
    )(adj, *folded)
    xva, coef_sens = call(
        functools.partial(last_kernel, n_scen, 1.0 / (scen * n_scen)),
        [struct((1, sets), f32), struct((chunk, cols), f32)],
        [VMEM] * (n_scen + 1),
        name="last",
    )(set_row, *chunks)
    return (xva.reshape(sets), coef_sens, feature_sens)


def solution(mesh):
    in_specs = (P("scen", None), P(), P(), P(None, "trade"), P("trade"), P("trade"), P(), P())
    out_specs = (P("trade"), P("scen", "trade"), P("trade", "scen"))
    return jax.shard_map(local, mesh=mesh, in_specs=in_specs, out_specs=out_specs, check_vma=False)
```

```python
import functools

import jax
import jax.numpy as jnp
from jax import lax
from jax.experimental import pallas as pl
from jax.experimental.pallas import tpu as pltpu
from jax.sharding import PartitionSpec as P

MAXDEG = 12
SET_SIZE = 16
INFO = 8
BLOCK = 128

f32 = jnp.float32
bf16 = jnp.bfloat16
VMEM = pl.BlockSpec(memory_space=pltpu.VMEM)
ANY = pl.BlockSpec(memory_space=pl.ANY)


def split(value):
    high = value.astype(bf16)
    low = (value - high.astype(f32)).astype(bf16)
    return high, low


def nn(left, right):
    return lax.dot_general(left, right, (((1,), (0,)), ((), ())), preferred_element_type=f32)


def nt(left, right):
    return lax.dot_general(left, right, (((1,), (1,)), ((), ())), preferred_element_type=f32)


def pair_nn(left, right):
    cols = right[0].shape[1]
    both = nn(left[0], jnp.concatenate(right, axis=1))
    return both[:, :cols] + both[:, cols:] + nn(left[1], right[0])


def iota(shape, dim):
    return lax.broadcasted_iota(jnp.int32, shape, dim)


def column(row):
    n = row.shape[1]
    return jnp.transpose(jnp.broadcast_to(row.astype(f32), (n, n)))


def one_hot(test):
    return jnp.where(test, f32(1), f32(0)).astype(bf16)


def pick(table, ids):
    rows, lanes = table.shape
    total = jnp.zeros((1, ids.shape[1]), f32)
    for r in range(rows):
        here = column(table[r : r + 1, :])
        where = iota((lanes, ids.shape[1]), 0) + r * lanes == ids
        total = total + jnp.sum(jnp.where(where, here[:, : ids.shape[1]], 0.0), axis=0, keepdims=True)
    return total


def basis(points):
    before, current = jnp.ones_like(points), points
    rows = [current]
    for _ in range(2, MAXDEG + 1):
        before, current = current, 2.0 * points * current - before
        rows.append(current)
    return jnp.concatenate(rows, axis=0)


def first_kernel(n_trade, *refs):
    ins, rest = refs[:8], refs[8:]
    folded_refs, rest = rest[:n_trade], rest[n_trade:]
    expo_ref, fact_out, key_out, side_out, member_out = rest[:5]
    fact_ref, factor_ref, degree_ref, set_ref, party_ref, thr_ref, wgt_ref, coef_buf, grid_ref, small, sems = rest[5:]
    fact_hbm, factor_hbm, degree_hbm, coef_hbm, set_hbm, party_hbm, thr_hbm, wgt_hbm = ins
    me = lax.axis_index("trade")
    width, cols = coef_hbm.shape
    sets = cols // SET_SIZE
    nfac, scen = fact_ref.shape
    own = width // n_trade
    steps = width // BLOCK
    per = own // BLOCK

    loads = [
        pltpu.make_async_copy(source, target, small.at[i])
        for i, (source, target) in enumerate(
            [
                (fact_hbm, fact_ref),
                (set_hbm, set_ref),
                (factor_hbm, factor_ref),
                (degree_hbm, degree_ref),
                (party_hbm, party_ref),
                (thr_hbm, thr_ref),
                (wgt_hbm, wgt_ref),
            ]
        )
    ]

    def start_row(step):
        return pl.multiple_of((me ^ (step // per)) * own + (step % per) * BLOCK, BLOCK)

    def copy(step):
        return pltpu.make_async_copy(
            coef_hbm.at[pl.ds(start_row(step), BLOCK), :], coef_buf.at[step], sems.at[step]
        )

    for load in loads:
        load.start()
    for step in range(steps):
        copy(step).start()
    for load in loads:
        load.wait()
    member = jnp.where(set_ref[...] - me * sets == iota((sets, cols), 0), f32(1), f32(0))
    member_out[...] = member.astype(bf16)
    turned_member = jnp.transpose(member).astype(bf16)
    fact_out[...] = fact_ref[...]
    table = split(jnp.transpose(basis(fact_ref[...])))
    key_out[...] = factor_ref[...] + nfac * (degree_ref[...] - 1)
    party = party_ref[...]
    thr_row = pick(thr_ref[...], party)
    wgt_row = pick(wgt_ref[...], party)
    line = iota((INFO, sets), 0)
    expo_ref[scen:, :] = jnp.where(line == 0, party.astype(f32), jnp.where(line == 1, thr_row, wgt_row))
    side_out[...] = jnp.where(line == 0, thr_ref[pl.ds(me, 1), :], wgt_ref[pl.ds(me, 1), :])
    for pair in range(steps // 2):
        highs, lows, keys = [], [], []
        for step in (2 * pair, 2 * pair + 1):
            copy(step).wait()
            coef_high, coef_low = split(coef_buf[step])
            folded = nn(coef_high, turned_member) + nn(coef_low, turned_member)
            folded_refs[step // per][pl.ds((step % per) * BLOCK, BLOCK), :] = folded
            high, low = split(folded)
            highs.append(high)
            lows.append(low)
            keys.append(key_out[pl.ds(lax.div(start_row(step), BLOCK), 1), :])
        right = jnp.concatenate([jnp.concatenate(highs, axis=0), jnp.concatenate(lows, axis=0)], axis=1)
        chosen = one_hot(iota((MAXDEG * nfac, 2 * BLOCK), 0) == jnp.concatenate(keys, axis=1))
        part = nn(chosen, right)
        grid_ref[...] = part if pair == 0 else grid_ref[...] + part
    expo_ref[:scen, :] = pair_nn(table, split(grid_ref[:, :sets] + grid_ref[:, sets:]))


def blocks_of(all_ref, n_trade):
    stride = all_ref.shape[0] // n_trade
    scen = stride - INFO
    expo = [split(all_ref[a * stride : a * stride + scen, :]) for a in range(n_trade)]
    pieces = tuple(jnp.concatenate([e[i] for e in expo], axis=1) for i in range(2))
    columns = [column(all_ref[a * stride + scen : a * stride + scen + 1, :]) for a in range(n_trade)]
    return pieces, columns


def same_as(columns, row):
    return one_hot(jnp.concatenate([here == row for here in columns], axis=0))


def info_of(all_ref, n_trade, block):
    stride = all_ref.shape[0] // n_trade
    info = all_ref[pl.ds(pl.multiple_of(block * stride + stride - INFO, INFO), INFO), :]
    return info[0:1, :], info[1:2, :], info[2:3, :]


def second_kernel(n_trade, all_ref, side_ref, fact_ref, msg_ref):
    trade = lax.axis_index("trade")
    sets = all_ref.shape[1]
    scen = all_ref.shape[0] // n_trade - INFO
    (high, low), columns = blocks_of(all_ref, n_trade)
    party, thr, wgt = info_of(all_ref, n_trade, trade)
    mine = (iota((1, sets), 1) + trade * sets).astype(f32)
    right = jnp.concatenate([same_as(columns, party), same_as(columns, mine)], axis=1)
    netted = nn(high, right) + nn(low, right)
    msg_ref[:scen, :] = wgt * jax.nn.sigmoid(netted[:, :sets] - thr)
    soft = jax.nn.softplus(netted[:, sets:] - side_ref[0:1, :])
    msg_ref[scen : scen + INFO, :] = jnp.broadcast_to(
        jnp.sum(soft, axis=0, keepdims=True) * side_ref[1:2, :], (INFO, sets)
    )
    nfac, base = fact_ref.shape[0], scen + INFO
    for piece in range(scen // sets):
        msg_ref[base + piece * nfac : base + (piece + 1) * nfac, :] = fact_ref[:, piece * sets : (piece + 1) * sets]


def response(msg_ref, nfac, scen):
    base = scen + INFO
    pieces = (msg_ref.shape[0] - base) // nfac
    points = jnp.concatenate(
        [msg_ref[base + i * nfac : base + (i + 1) * nfac, :] for i in range(pieces)], axis=1
    )
    return pair_nn(split(basis(points)), split(msg_ref[:scen, :]))


def middle_kernel(n_scen, nfac, scen, msg_ref, key_ref, grid_ref, chosen_ref, column_ref):
    me = lax.axis_index("scen")
    lines = key_ref.shape[0]
    chunk = lines * BLOCK // n_scen
    for i in range(lines):
        column_ref[i * BLOCK : (i + 1) * BLOCK, :] = column(key_ref[i : i + 1, :])
    rows = grid_ref.shape[0]
    for j in range(n_scen // 2):
        here = column_ref[pl.ds(pl.multiple_of((me ^ (2 * j)) * chunk, chunk), chunk), :].astype(jnp.int32)
        for i in range(rows // BLOCK):
            chosen_ref[j * chunk : (j + 1) * chunk, i * BLOCK : (i + 1) * BLOCK] = one_hot(
                here == iota(here.shape, 1) + i * BLOCK
            )
    grid_ref[...] = response(msg_ref, nfac, scen)


def third_kernel(n_scen, nfac, scen, msg_ref, own_ref, grid_ref, chosen_ref, *chunk_refs):
    chunk = chosen_ref.shape[0] // len(chunk_refs)
    both = jnp.concatenate(split(grid_ref[...] + response(msg_ref, nfac, scen)), axis=1)
    xva = msg_ref[scen : scen + INFO, :] + own_ref[scen : scen + INFO, :]
    sets = msg_ref.shape[1]
    for j, ref in enumerate(chunk_refs):
        part = nn(chosen_ref[j * chunk : (j + 1) * chunk, :], both)
        ref[:chunk, :] = part[:, :sets] + part[:, sets:]
        ref[chunk:, :] = xva


def feature_kernel(n_trade, all_ref, *refs):
    folded_refs, out_ref = refs[:n_trade], refs[n_trade]
    trade = lax.axis_index("trade")
    (high, low), columns = blocks_of(all_ref, n_trade)
    total = jnp.zeros(out_ref.shape, f32)
    for k in range(n_trade):
        party, thr, wgt = info_of(all_ref, n_trade, trade ^ k)
        same = same_as(columns, party)
        netted = nn(high, same) + nn(low, same)
        adj_high, adj_low = split(wgt * jax.nn.sigmoid(netted - thr))
        fold_high, fold_low = split(folded_refs[k][...])
        total = total + nt(fold_high, adj_high) + nt(fold_low, adj_high) + nt(fold_high, adj_low)
    out_ref[...] = total


def last_kernel(n_chunks, scale, member_ref, *refs):
    chunk_refs, (xva_hbm, out_hbm, xva_ref, out_ref, sems) = refs[:n_chunks], refs[n_chunks:]
    rows, cols = out_hbm.shape
    total = chunk_refs[0][...]
    for ref in chunk_refs[1:]:
        total = total + ref[...]
    total = total * scale
    xva_ref[...] = total[rows : rows + 1, :]
    first = pltpu.make_async_copy(xva_ref, xva_hbm, sems.at[0])
    first.start()
    high, low = split(total[:rows, :])
    copies = [first]
    pieces = sems.shape[0] - 1
    wide = cols // pieces
    for i in range(pieces):
        part = member_ref[:, i * wide : (i + 1) * wide]
        out_ref[:, i * wide : (i + 1) * wide] = nn(high, part) + nn(low, part)
        copies.append(
            pltpu.make_async_copy(
                out_ref.at[:, pl.ds(i * wide, wide)], out_hbm.at[:, pl.ds(i * wide, wide)], sems.at[i + 1]
            )
        )
        copies[-1].start()
    for copy in copies:
        copy.wait()


def call(kernel, out_shape, in_specs, args, name, scratch=(), flops=5 * 10**8, limit=None):
    args = [
        pltpu.with_memory_space_constraint(arg, pltpu.VMEM) if spec is VMEM else arg
        for arg, spec in zip(args, in_specs)
    ]
    specs = [ANY if isinstance(shape, jax.ShapeDtypeStruct) else VMEM for shape in out_shape]
    return pl.pallas_call(
        kernel,
        out_shape=out_shape,
        in_specs=in_specs,
        out_specs=specs,
        scratch_shapes=scratch,
        cost_estimate=pl.CostEstimate(flops=flops, bytes_accessed=10**5, transcendentals=0),
        compiler_params=pltpu.CompilerParams(vmem_limit_bytes=limit),
        name=name,
    )(*args)


def local(
    factors, feat_factor, feat_degree, coefficients, set_of_trade, party_of_set, threshold, weight
):
    n_trade, n_scen = lax.axis_size("trade"), lax.axis_size("scen")
    scen, nfac = factors.shape
    width, cols = coefficients.shape
    sets = cols // SET_SIZE
    lines = width // BLOCK
    own, chunk, grid = width // n_trade, width // n_scen, MAXDEG * nfac
    struct, vmem, dma = jax.ShapeDtypeStruct, pltpu.VMEM, pltpu.SemaphoreType.DMA
    i32 = jnp.int32
    outs = call(
        functools.partial(first_kernel, n_trade),
        [vmem((own, sets), f32)] * n_trade
        + [vmem((scen + INFO, sets), f32), vmem((nfac, scen), f32), vmem((lines, BLOCK), i32)]
        + [vmem((INFO, sets), f32), vmem((sets, cols), bf16)],
        [ANY] * 8,
        [
            factors.T,
            feat_factor.reshape(lines, BLOCK),
            feat_degree.reshape(lines, BLOCK),
            coefficients,
            set_of_trade.reshape(1, cols),
            party_of_set.reshape(1, sets),
            threshold.reshape(n_trade, sets),
            weight.reshape(n_trade, sets),
        ],
        "first",
        [
            vmem((nfac, scen), f32),
            vmem((lines, BLOCK), i32),
            vmem((lines, BLOCK), i32),
            vmem((1, cols), i32),
            vmem((1, sets), i32),
            vmem((n_trade, sets), f32),
            vmem((n_trade, sets), f32),
            vmem((lines, BLOCK, cols), f32),
            vmem((grid, 2 * sets), f32),
            dma((7,)),
            dma((lines,)),
        ],
        limit=32 << 20,
    )
    folded, (expo, fact, key, side, member) = outs[:n_trade], outs[n_trade:]
    everything = lax.all_gather(expo, "trade", axis=0, tiled=True)
    (msg,) = call(
        functools.partial(second_kernel, n_trade),
        [vmem((scen + INFO + nfac * scen // sets, sets), f32)],
        [VMEM] * 3,
        [everything, side, fact],
        "second",
        limit=8 << 20,
    )
    peer = lax.ppermute(msg, "scen", [(i, i ^ 1) for i in range(n_scen)])
    half, chosen = call(
        functools.partial(middle_kernel, n_scen, nfac, scen),
        [vmem((grid, sets), f32), vmem((width // 2, grid), bf16)],
        [VMEM] * 2,
        [msg, key],
        "middle",
        [vmem((width, BLOCK), f32)],
        limit=8 << 20,
    )
    msg, *later = lax.optimization_barrier((msg, *folded[1:]))
    moved = [folded[0]] + [
        lax.ppermute(later[k - 1], "trade", [(i, i ^ k) for i in range(n_trade)])
        for k in range(1, n_trade)
    ]
    chunks = call(
        functools.partial(third_kernel, n_scen, nfac, scen),
        [vmem((chunk + INFO, sets), f32)] * (n_scen // 2),
        [VMEM] * 4,
        [peer, msg, half, chosen],
        "third",
        limit=8 << 20,
    )
    chunks = [chunks[0]] + [
        lax.ppermute(chunks[j], "scen", [(i, i ^ (2 * j)) for i in range(n_scen)])
        for j in range(n_scen // 2 - 1, 0, -1)
    ]
    (feature_sens,) = call(
        functools.partial(feature_kernel, n_trade),
        [vmem((own, scen), f32)],
        [VMEM] * (n_trade + 1),
        [everything, *moved],
        "feature",
        flops=2 * 10**9,
        limit=8 << 20,
    )
    xva, coef_sens = call(
        functools.partial(last_kernel, n_scen // 2, 1.0 / (scen * n_scen)),
        [struct((1, sets), f32), struct((chunk, cols), f32)],
        [VMEM] * (n_scen // 2 + 1),
        [member, *chunks],
        "last",
        [vmem((1, sets), f32), vmem((chunk, cols), f32), dma((5,))],
        limit=8 << 20,
    )
    return (xva.reshape(sets), coef_sens, feature_sens)


def solution(mesh):
    in_specs = (P("scen", None), P(), P(), P(None, "trade"), P("trade"), P("trade"), P(), P())
    out_specs = (P("trade"), P("scen", "trade"), P("trade", "scen"))
    return jax.shard_map(local, mesh=mesh, in_specs=in_specs, out_specs=out_specs, check_vma=False)
```

```python
import functools

import jax
import jax.numpy as jnp
from jax import lax
from jax.experimental import pallas as pl
from jax.experimental.pallas import tpu as pltpu
from jax.sharding import PartitionSpec as P

MAXDEG = 12
SET_SIZE = 16
INFO = 8
BLOCK = 128

f32 = jnp.float32
bf16 = jnp.bfloat16
VMEM = pl.BlockSpec(memory_space=pltpu.VMEM)
HBM = pl.BlockSpec(memory_space=pltpu.HBM)


def split(value):
    high = value.astype(bf16)
    low = (value - high.astype(f32)).astype(bf16)
    return high, low


def nn(left, right):
    return lax.dot_general(left, right, (((1,), (0,)), ((), ())), preferred_element_type=f32)


def nt(left, right):
    return lax.dot_general(left, right, (((1,), (1,)), ((), ())), preferred_element_type=f32)


def pair_nn(left, right):
    cols = right[0].shape[1]
    both = nn(left[0], jnp.concatenate(right, axis=1))
    return both[:, :cols] + both[:, cols:] + nn(left[1], right[0])


def iota(shape, dim):
    return lax.broadcasted_iota(jnp.int32, shape, dim)


def column(row):
    n = row.shape[1]
    return jnp.transpose(jnp.broadcast_to(row.astype(f32), (n, n)))


def one_hot(test):
    return jnp.where(test, f32(1), f32(0)).astype(bf16)


def pick(table, ids):
    rows, lanes = table.shape
    total = jnp.zeros((1, ids.shape[1]), f32)
    for r in range(rows):
        here = column(table[r : r + 1, :])
        where = iota((lanes, ids.shape[1]), 0) + r * lanes == ids
        total = total + jnp.sum(jnp.where(where, here[:, : ids.shape[1]], 0.0), axis=0, keepdims=True)
    return total


def basis(points):
    before, current = jnp.ones_like(points), points
    rows = [current]
    for _ in range(2, MAXDEG + 1):
        before, current = current, 2.0 * points * current - before
        rows.append(current)
    return jnp.concatenate(rows, axis=0)


def first_kernel(n_trade, *refs):
    ins, rest = refs[:8], refs[8:]
    folded_refs, rest = rest[:n_trade], rest[n_trade:]
    expo_ref, fact_out, key_out, side_out, member_out = rest[:5]
    fact_ref, factor_ref, degree_ref, set_ref, party_ref, thr_ref, wgt_ref, coef_buf, grid_ref, small, sems = rest[5:]
    fact_hbm, factor_hbm, degree_hbm, coef_hbm, set_hbm, party_hbm, thr_hbm, wgt_hbm = ins
    me = lax.axis_index("trade")
    width, cols = coef_hbm.shape
    sets = cols // SET_SIZE
    nfac, scen = fact_ref.shape
    own = width // n_trade
    steps = width // BLOCK
    per = own // BLOCK

    loads = [
        pltpu.make_async_copy(source, target, small.at[i])
        for i, (source, target) in enumerate(
            [
                (fact_hbm, fact_ref),
                (set_hbm, set_ref),
                (factor_hbm, factor_ref),
                (degree_hbm, degree_ref),
                (party_hbm, party_ref),
                (thr_hbm, thr_ref),
                (wgt_hbm, wgt_ref),
            ]
        )
    ]

    def start_row(step):
        return pl.multiple_of((me ^ (step // per)) * own + (step % per) * BLOCK, BLOCK)

    def copy(step):
        return pltpu.make_async_copy(
            coef_hbm.at[pl.ds(start_row(step), BLOCK), :], coef_buf.at[step], sems.at[step]
        )

    for load in loads:
        load.start()
    for step in range(steps):
        copy(step).start()
    for load in loads:
        load.wait()
    member = jnp.where(set_ref[...] - me * sets == iota((sets, cols), 0), f32(1), f32(0))
    member_out[...] = member.astype(bf16)
    turned_member = jnp.transpose(member).astype(bf16)
    fact_out[...] = fact_ref[...]
    table = split(jnp.transpose(basis(fact_ref[...])))
    key_out[...] = factor_ref[...] + nfac * (degree_ref[...] - 1)
    party = party_ref[...]
    thr_row = pick(thr_ref[...], party)
    wgt_row = pick(wgt_ref[...], party)
    line = iota((INFO, sets), 0)
    expo_ref[scen:, :] = jnp.where(line == 0, party.astype(f32), jnp.where(line == 1, thr_row, wgt_row))
    side_out[...] = jnp.where(line == 0, thr_ref[pl.ds(me, 1), :], wgt_ref[pl.ds(me, 1), :])
    for pair in range(steps // 2):
        highs, lows, keys = [], [], []
        for step in (2 * pair, 2 * pair + 1):
            copy(step).wait()
            coef_high, coef_low = split(coef_buf[step])
            folded = nn(coef_high, turned_member) + nn(coef_low, turned_member)
            folded_refs[step // per][pl.ds((step % per) * BLOCK, BLOCK), :] = folded
            high, low = split(folded)
            highs.append(high)
            lows.append(low)
            keys.append(key_out[pl.ds(lax.div(start_row(step), BLOCK), 1), :])
        right = jnp.concatenate([jnp.concatenate(highs, axis=0), jnp.concatenate(lows, axis=0)], axis=1)
        chosen = one_hot(iota((MAXDEG * nfac, 2 * BLOCK), 0) == jnp.concatenate(keys, axis=1))
        part = nn(chosen, right)
        grid_ref[...] = part if pair == 0 else grid_ref[...] + part
    expo_ref[:scen, :] = pair_nn(table, split(grid_ref[:, :sets] + grid_ref[:, sets:]))


def blocks_of(all_ref, n_trade):
    stride = all_ref.shape[0] // n_trade
    scen = stride - INFO
    expo = [split(all_ref[a * stride : a * stride + scen, :]) for a in range(n_trade)]
    pieces = tuple(jnp.concatenate([e[i] for e in expo], axis=1) for i in range(2))
    columns = [column(all_ref[a * stride + scen : a * stride + scen + 1, :]) for a in range(n_trade)]
    return pieces, columns


def same_as(columns, row):
    return one_hot(jnp.concatenate([here == row for here in columns], axis=0))


def info_of(all_ref, n_trade, block):
    stride = all_ref.shape[0] // n_trade
    info = all_ref[pl.ds(pl.multiple_of(block * stride + stride - INFO, INFO), INFO), :]
    return info[0:1, :], info[1:2, :], info[2:3, :]


def second_kernel(n_trade, all_ref, side_ref, fact_ref, msg_ref):
    trade = lax.axis_index("trade")
    sets = all_ref.shape[1]
    scen = all_ref.shape[0] // n_trade - INFO
    (high, low), columns = blocks_of(all_ref, n_trade)
    party, thr, wgt = info_of(all_ref, n_trade, trade)
    mine = (iota((1, sets), 1) + trade * sets).astype(f32)
    right = jnp.concatenate([same_as(columns, party), same_as(columns, mine)], axis=1)
    netted = nn(high, right) + nn(low, right)
    msg_ref[:scen, :] = wgt * jax.nn.sigmoid(netted[:, :sets] - thr)
    soft = jax.nn.softplus(netted[:, sets:] - side_ref[0:1, :])
    msg_ref[scen : scen + INFO, :] = jnp.broadcast_to(
        jnp.sum(soft, axis=0, keepdims=True) * side_ref[1:2, :], (INFO, sets)
    )
    nfac, base = fact_ref.shape[0], scen + INFO
    for piece in range(scen // sets):
        msg_ref[base + piece * nfac : base + (piece + 1) * nfac, :] = fact_ref[:, piece * sets : (piece + 1) * sets]


def response(msg_ref, nfac, scen):
    base = scen + INFO
    pieces = (msg_ref.shape[0] - base) // nfac
    points = jnp.concatenate(
        [msg_ref[base + i * nfac : base + (i + 1) * nfac, :] for i in range(pieces)], axis=1
    )
    return pair_nn(split(basis(points)), split(msg_ref[:scen, :]))


def middle_kernel(n_scen, nfac, scen, msg_ref, key_ref, grid_ref, chosen_ref, column_ref):
    me = lax.axis_index("scen")
    lines = key_ref.shape[0]
    chunk = lines * BLOCK // n_scen
    for i in range(lines):
        column_ref[i * BLOCK : (i + 1) * BLOCK, :] = column(key_ref[i : i + 1, :])
    rows = grid_ref.shape[0]
    for j in range(n_scen // 2):
        here = column_ref[pl.ds(pl.multiple_of((me ^ (2 * j)) * chunk, chunk), chunk), :].astype(jnp.int32)
        for i in range(rows // BLOCK):
            chosen_ref[j * chunk : (j + 1) * chunk, i * BLOCK : (i + 1) * BLOCK] = one_hot(
                here == iota(here.shape, 1) + i * BLOCK
            )
    grid_ref[...] = response(msg_ref, nfac, scen)


def third_kernel(n_scen, nfac, scen, msg_ref, own_ref, grid_ref, chosen_ref, *chunk_refs):
    chunk = chosen_ref.shape[0] // len(chunk_refs)
    both = jnp.concatenate(split(grid_ref[...] + response(msg_ref, nfac, scen)), axis=1)
    xva = msg_ref[scen : scen + INFO, :] + own_ref[scen : scen + INFO, :]
    sets = msg_ref.shape[1]
    for j, ref in enumerate(chunk_refs):
        part = nn(chosen_ref[j * chunk : (j + 1) * chunk, :], both)
        ref[:chunk, :] = part[:, :sets] + part[:, sets:]
        ref[chunk:, :] = xva


def feature_kernel(n_trade, all_ref, *refs):
    folded_refs, (out_hbm, out_ref, sem) = refs[:n_trade], refs[n_trade:]
    trade = lax.axis_index("trade")
    (high, low), columns = blocks_of(all_ref, n_trade)
    total = jnp.zeros(out_ref.shape, f32)
    for k in range(n_trade):
        party, thr, wgt = info_of(all_ref, n_trade, trade ^ k)
        same = same_as(columns, party)
        netted = nn(high, same) + nn(low, same)
        adj_high, adj_low = split(wgt * jax.nn.sigmoid(netted - thr))
        fold_high, fold_low = split(folded_refs[k][...])
        total = total + nt(fold_high, adj_high) + nt(fold_low, adj_high) + nt(fold_high, adj_low)
    out_ref[...] = total
    copy = pltpu.make_async_copy(out_ref, out_hbm, sem)
    copy.start()
    copy.wait()


def last_kernel(n_chunks, scale, member_ref, *refs):
    chunk_refs, (xva_hbm, out_hbm, xva_ref, out_ref, sems) = refs[:n_chunks], refs[n_chunks:]
    rows, cols = out_hbm.shape
    total = chunk_refs[0][...]
    for ref in chunk_refs[1:]:
        total = total + ref[...]
    total = total * scale
    xva_ref[...] = total[rows : rows + 1, :]
    first = pltpu.make_async_copy(xva_ref, xva_hbm, sems.at[0])
    first.start()
    high, low = split(total[:rows, :])
    copies = [first]
    pieces = sems.shape[0] - 1
    wide = cols // pieces
    for i in range(pieces):
        part = member_ref[:, i * wide : (i + 1) * wide]
        out_ref[:, i * wide : (i + 1) * wide] = nn(high, part) + nn(low, part)
        copies.append(
            pltpu.make_async_copy(
                out_ref.at[:, pl.ds(i * wide, wide)], out_hbm.at[:, pl.ds(i * wide, wide)], sems.at[i + 1]
            )
        )
        copies[-1].start()
    for copy in copies:
        copy.wait()


def call(kernel, out_shape, in_specs, args, name, scratch=(), flops=5 * 10**8, limit=None):
    args = [
        pltpu.with_memory_space_constraint(arg, pltpu.VMEM if spec is VMEM else pltpu.HBM)
        for arg, spec in zip(args, in_specs)
    ]
    specs = [HBM if isinstance(shape, jax.ShapeDtypeStruct) else VMEM for shape in out_shape]
    return pl.pallas_call(
        kernel,
        out_shape=out_shape,
        in_specs=in_specs,
        out_specs=specs,
        scratch_shapes=scratch,
        cost_estimate=pl.CostEstimate(flops=flops, bytes_accessed=10**5, transcendentals=0),
        compiler_params=pltpu.CompilerParams(vmem_limit_bytes=limit),
        name=name,
    )(*args)


def local(
    factors, feat_factor, feat_degree, coefficients, set_of_trade, party_of_set, threshold, weight
):
    n_trade, n_scen = lax.axis_size("trade"), lax.axis_size("scen")
    scen, nfac = factors.shape
    width, cols = coefficients.shape
    sets = cols // SET_SIZE
    lines = width // BLOCK
    own, chunk, grid = width // n_trade, width // n_scen, MAXDEG * nfac
    struct, vmem, dma = jax.ShapeDtypeStruct, pltpu.VMEM, pltpu.SemaphoreType.DMA
    i32 = jnp.int32
    outs = call(
        functools.partial(first_kernel, n_trade),
        [vmem((own, sets), f32)] * n_trade
        + [vmem((scen + INFO, sets), f32), vmem((nfac, scen), f32), vmem((lines, BLOCK), i32)]
        + [vmem((INFO, sets), f32), vmem((sets, cols), bf16)],
        [HBM] * 8,
        [
            factors.T,
            feat_factor.reshape(lines, BLOCK),
            feat_degree.reshape(lines, BLOCK),
            coefficients,
            set_of_trade.reshape(1, cols),
            party_of_set.reshape(1, sets),
            threshold.reshape(n_trade, sets),
            weight.reshape(n_trade, sets),
        ],
        "first",
        [
            vmem((nfac, scen), f32),
            vmem((lines, BLOCK), i32),
            vmem((lines, BLOCK), i32),
            vmem((1, cols), i32),
            vmem((1, sets), i32),
            vmem((n_trade, sets), f32),
            vmem((n_trade, sets), f32),
            vmem((lines, BLOCK, cols), f32),
            vmem((grid, 2 * sets), f32),
            dma((7,)),
            dma((lines,)),
        ],
        limit=32 << 20,
    )
    folded, (expo, fact, key, side, member) = outs[:n_trade], outs[n_trade:]
    everything = lax.all_gather(expo, "trade", axis=0, tiled=True)
    (msg,) = call(
        functools.partial(second_kernel, n_trade),
        [vmem((scen + INFO + nfac * scen // sets, sets), f32)],
        [VMEM] * 3,
        [everything, side, fact],
        "second",
        limit=8 << 20,
    )
    peer = lax.ppermute(msg, "scen", [(i, i ^ 1) for i in range(n_scen)])
    half, chosen = call(
        functools.partial(middle_kernel, n_scen, nfac, scen),
        [vmem((grid, sets), f32), vmem((width // 2, grid), bf16)],
        [VMEM] * 2,
        [msg, key],
        "middle",
        [vmem((width, BLOCK), f32)],
        limit=8 << 20,
    )
    msg, *later = lax.optimization_barrier((msg, *folded[1:]))
    moved = [folded[0]] + [
        lax.ppermute(later[k - 1], "trade", [(i, i ^ k) for i in range(n_trade)])
        for k in range(1, n_trade)
    ]
    chunks = call(
        functools.partial(third_kernel, n_scen, nfac, scen),
        [vmem((chunk + INFO, sets), f32)] * (n_scen // 2),
        [VMEM] * 4,
        [peer, msg, half, chosen],
        "third",
        limit=8 << 20,
    )
    chunks = [chunks[0]] + [
        lax.ppermute(chunks[j], "scen", [(i, i ^ (2 * j)) for i in range(n_scen)])
        for j in range(n_scen // 2 - 1, 0, -1)
    ]
    (feature_sens,) = call(
        functools.partial(feature_kernel, n_trade),
        [struct((own, scen), f32)],
        [VMEM] * (n_trade + 1),
        [everything, *moved],
        "feature",
        [vmem((own, scen), f32), dma],
        flops=2 * 10**9,
        limit=8 << 20,
    )
    xva, coef_sens = call(
        functools.partial(last_kernel, n_scen // 2, 1.0 / (scen * n_scen)),
        [struct((1, sets), f32), struct((chunk, cols), f32)],
        [VMEM] * (n_scen // 2 + 1),
        [member, *chunks],
        "last",
        [vmem((1, sets), f32), vmem((chunk, cols), f32), dma((5,))],
        limit=8 << 20,
    )
    return (xva.reshape(sets), coef_sens, feature_sens)


def solution(mesh):
    in_specs = (P("scen", None), P(), P(), P(None, "trade"), P("trade"), P("trade"), P(), P())
    out_specs = (P("trade"), P("scen", "trade"), P("trade", "scen"))
    return jax.shard_map(local, mesh=mesh, in_specs=in_specs, out_specs=out_specs, check_vma=False)
```

```python
import functools

import jax
import jax.numpy as jnp
from jax import lax
from jax.experimental import pallas as pl
from jax.experimental.pallas import tpu as pltpu
from jax.sharding import PartitionSpec as P

MAXDEG = 12
SET_SIZE = 16
INFO = 8
BLOCK = 128

f32 = jnp.float32
bf16 = jnp.bfloat16
VMEM = pl.BlockSpec(memory_space=pltpu.VMEM)
HBM = pl.BlockSpec(memory_space=pltpu.HBM)


def split(value):
    high = value.astype(bf16)
    low = (value - high.astype(f32)).astype(bf16)
    return high, low


def nn(left, right):
    return lax.dot_general(left, right, (((1,), (0,)), ((), ())), preferred_element_type=f32)


def nt(left, right):
    return lax.dot_general(left, right, (((1,), (1,)), ((), ())), preferred_element_type=f32)


def pair_nn(left, right):
    cols = right[0].shape[1]
    both = nn(left[0], jnp.concatenate(right, axis=1))
    return both[:, :cols] + both[:, cols:] + nn(left[1], right[0])


def iota(shape, dim):
    return lax.broadcasted_iota(jnp.int32, shape, dim)


def column(row):
    n = row.shape[1]
    return jnp.transpose(jnp.broadcast_to(row.astype(f32), (n, n)))


def one_hot(test):
    return jnp.where(test, f32(1), f32(0)).astype(bf16)


def pick(table, ids):
    rows, lanes = table.shape
    total = jnp.zeros((1, ids.shape[1]), f32)
    for r in range(rows):
        here = column(table[r : r + 1, :])
        where = iota((lanes, ids.shape[1]), 0) + r * lanes == ids
        total = total + jnp.sum(jnp.where(where, here[:, : ids.shape[1]], 0.0), axis=0, keepdims=True)
    return total


def basis(points):
    before, current = jnp.ones_like(points), points
    rows = [current]
    for _ in range(2, MAXDEG + 1):
        before, current = current, 2.0 * points * current - before
        rows.append(current)
    return jnp.concatenate(rows, axis=0)


def first_kernel(n_trade, *refs):
    ins, rest = refs[:8], refs[8:]
    folded_refs, rest = rest[:n_trade], rest[n_trade:]
    expo_ref, fact_out, key_out, side_out, member_out = rest[:5]
    fact_ref, factor_ref, degree_ref, set_ref, party_ref, thr_ref, wgt_ref, coef_buf, small, sems = rest[5:]
    fact_hbm, factor_hbm, degree_hbm, coef_hbm, set_hbm, party_hbm, thr_hbm, wgt_hbm = ins
    me = lax.axis_index("trade")
    width, cols = coef_hbm.shape
    sets = cols // SET_SIZE
    nfac, scen = fact_ref.shape
    own = width // n_trade
    steps = width // BLOCK
    per = own // BLOCK

    loads = [
        pltpu.make_async_copy(source, target, small.at[i])
        for i, (source, target) in enumerate(
            [
                (fact_hbm, fact_ref),
                (set_hbm, set_ref),
                (factor_hbm, factor_ref),
                (degree_hbm, degree_ref),
                (party_hbm, party_ref),
                (thr_hbm, thr_ref),
                (wgt_hbm, wgt_ref),
            ]
        )
    ]

    def start_row(step):
        return pl.multiple_of((me ^ (step // per)) * own + (step % per) * BLOCK, BLOCK)

    def copy(step):
        return pltpu.make_async_copy(
            coef_hbm.at[pl.ds(start_row(step), BLOCK), :], coef_buf.at[step], sems.at[step]
        )

    for load in loads:
        load.start()
    for step in range(steps):
        copy(step).start(priority=1)
    for load in loads:
        load.wait()
    member = jnp.where(set_ref[...] - me * sets == iota((sets, cols), 0), f32(1), f32(0))
    member_out[...] = member.astype(bf16)
    turned_member = jnp.transpose(member).astype(bf16)
    fact_out[...] = fact_ref[...]
    table = split(jnp.transpose(basis(fact_ref[...])))
    key_out[...] = factor_ref[...] + nfac * (degree_ref[...] - 1)
    party = party_ref[...]
    thr_row = pick(thr_ref[...], party)
    wgt_row = pick(wgt_ref[...], party)
    line = iota((INFO, sets), 0)
    expo_ref[scen:, :] = jnp.where(line == 0, party.astype(f32), jnp.where(line == 1, thr_row, wgt_row))
    side_out[...] = jnp.where(line == 0, thr_ref[pl.ds(me, 1), :], wgt_ref[pl.ds(me, 1), :])
    keys = [key_out[pl.ds(lax.div(start_row(step), BLOCK), 1), :] for step in range(steps)]
    chosen = one_hot(iota((MAXDEG * nfac, width), 0) == jnp.concatenate(keys, axis=1))
    phi = [nn(part, chosen).astype(bf16) for part in table]
    done, total = 0, None
    for size in (steps // 2, steps - steps // 2):
        group = range(done, done + size)
        for step in group:
            copy(step).wait()
        highs, lows = [], []
        for step in group:
            coef_high, coef_low = split(coef_buf[step])
            folded = nn(coef_high, turned_member) + nn(coef_low, turned_member)
            folded_refs[step // per][pl.ds((step % per) * BLOCK, BLOCK), :] = folded
            high, low = split(folded)
            highs.append(high)
            lows.append(low)
        here = slice(done * BLOCK, (done + size) * BLOCK)
        part = pair_nn(
            [piece[:, here] for piece in phi],
            [jnp.concatenate(highs, axis=0), jnp.concatenate(lows, axis=0)],
        )
        total = part if total is None else total + part
        done += size
    expo_ref[:scen, :] = total


def blocks_of(all_ref, n_trade):
    stride = all_ref.shape[0] // n_trade
    scen = stride - INFO
    expo = [split(all_ref[a * stride : a * stride + scen, :]) for a in range(n_trade)]
    pieces = tuple(jnp.concatenate([e[i] for e in expo], axis=1) for i in range(2))
    columns = [column(all_ref[a * stride + scen : a * stride + scen + 1, :]) for a in range(n_trade)]
    return pieces, columns


def same_as(columns, row):
    return one_hot(jnp.concatenate([here == row for here in columns], axis=0))


def info_of(all_ref, n_trade, block):
    stride = all_ref.shape[0] // n_trade
    info = all_ref[pl.ds(pl.multiple_of(block * stride + stride - INFO, INFO), INFO), :]
    return info[0:1, :], info[1:2, :], info[2:3, :]


def second_kernel(n_trade, all_ref, side_ref, fact_ref, msg_ref):
    trade = lax.axis_index("trade")
    sets = all_ref.shape[1]
    scen = all_ref.shape[0] // n_trade - INFO
    (high, low), columns = blocks_of(all_ref, n_trade)
    party, thr, wgt = info_of(all_ref, n_trade, trade)
    mine = (iota((1, sets), 1) + trade * sets).astype(f32)
    right = jnp.concatenate([same_as(columns, party), same_as(columns, mine)], axis=1)
    netted = nn(high, right) + nn(low, right)
    msg_ref[:scen, :] = wgt * jax.nn.sigmoid(netted[:, :sets] - thr)
    soft = jax.nn.softplus(netted[:, sets:] - side_ref[0:1, :])
    msg_ref[scen : scen + INFO, :] = jnp.broadcast_to(
        jnp.sum(soft, axis=0, keepdims=True) * side_ref[1:2, :], (INFO, sets)
    )
    nfac, base = fact_ref.shape[0], scen + INFO
    for piece in range(scen // sets):
        msg_ref[base + piece * nfac : base + (piece + 1) * nfac, :] = fact_ref[:, piece * sets : (piece + 1) * sets]


def response(msg_ref, nfac, scen):
    base = scen + INFO
    pieces = (msg_ref.shape[0] - base) // nfac
    points = jnp.concatenate(
        [msg_ref[base + i * nfac : base + (i + 1) * nfac, :] for i in range(pieces)], axis=1
    )
    return pair_nn(split(basis(points)), split(msg_ref[:scen, :]))


def middle_kernel(n_scen, nfac, scen, msg_ref, key_ref, grid_ref, chosen_ref, column_ref):
    me = lax.axis_index("scen")
    lines = key_ref.shape[0]
    chunk = lines * BLOCK // n_scen
    for i in range(lines):
        column_ref[i * BLOCK : (i + 1) * BLOCK, :] = column(key_ref[i : i + 1, :])
    rows = grid_ref.shape[0]
    for j in range(n_scen // 2):
        here = column_ref[pl.ds(pl.multiple_of((me ^ (2 * j)) * chunk, chunk), chunk), :].astype(jnp.int32)
        for i in range(rows // BLOCK):
            chosen_ref[j * chunk : (j + 1) * chunk, i * BLOCK : (i + 1) * BLOCK] = one_hot(
                here == iota(here.shape, 1) + i * BLOCK
            )
    grid_ref[...] = response(msg_ref, nfac, scen)


def third_kernel(n_scen, nfac, scen, msg_ref, own_ref, grid_ref, chosen_ref, *chunk_refs):
    chunk = chosen_ref.shape[0] // len(chunk_refs)
    both = jnp.concatenate(split(grid_ref[...] + response(msg_ref, nfac, scen)), axis=1)
    xva = msg_ref[scen : scen + INFO, :] + own_ref[scen : scen + INFO, :]
    sets = msg_ref.shape[1]
    for j, ref in enumerate(chunk_refs):
        part = nn(chosen_ref[j * chunk : (j + 1) * chunk, :], both)
        ref[:chunk, :] = part[:, :sets] + part[:, sets:]
        ref[chunk:, :] = xva


def feature_kernel(n_trade, all_ref, *refs):
    folded_refs, (out_hbm, out_ref, sem) = refs[:n_trade], refs[n_trade:]
    trade = lax.axis_index("trade")
    (high, low), columns = blocks_of(all_ref, n_trade)
    total = jnp.zeros(out_ref.shape, f32)
    for k in range(n_trade):
        party, thr, wgt = info_of(all_ref, n_trade, trade ^ k)
        same = same_as(columns, party)
        netted = nn(high, same) + nn(low, same)
        adj_high, adj_low = split(wgt * jax.nn.sigmoid(netted - thr))
        fold_high, fold_low = split(folded_refs[k][...])
        total = total + nt(fold_high, adj_high) + nt(fold_low, adj_high) + nt(fold_high, adj_low)
    out_ref[...] = total
    copy = pltpu.make_async_copy(out_ref, out_hbm, sem)
    copy.start()
    copy.wait()


def last_kernel(n_chunks, scale, member_ref, *refs):
    chunk_refs, (xva_hbm, out_hbm, xva_ref, out_ref, sems) = refs[:n_chunks], refs[n_chunks:]
    rows, cols = out_hbm.shape
    total = chunk_refs[0][...]
    for ref in chunk_refs[1:]:
        total = total + ref[...]
    total = total * scale
    xva_ref[...] = total[rows : rows + 1, :]
    first = pltpu.make_async_copy(xva_ref, xva_hbm, sems.at[0])
    first.start()
    high, low = split(total[:rows, :])
    copies = [first]
    pieces = sems.shape[0] - 1
    wide = cols // pieces
    for i in range(pieces):
        part = member_ref[:, i * wide : (i + 1) * wide]
        out_ref[:, i * wide : (i + 1) * wide] = nn(high, part) + nn(low, part)
        copies.append(
            pltpu.make_async_copy(
                out_ref.at[:, pl.ds(i * wide, wide)], out_hbm.at[:, pl.ds(i * wide, wide)], sems.at[i + 1]
            )
        )
        copies[-1].start()
    for copy in copies:
        copy.wait()


def call(kernel, out_shape, in_specs, args, name, scratch=(), flops=5 * 10**8, limit=None):
    args = [
        pltpu.with_memory_space_constraint(arg, pltpu.VMEM if spec is VMEM else pltpu.HBM)
        for arg, spec in zip(args, in_specs)
    ]
    specs = [HBM if isinstance(shape, jax.ShapeDtypeStruct) else VMEM for shape in out_shape]
    return pl.pallas_call(
        kernel,
        out_shape=out_shape,
        in_specs=in_specs,
        out_specs=specs,
        scratch_shapes=scratch,
        cost_estimate=pl.CostEstimate(flops=flops, bytes_accessed=10**5, transcendentals=0),
        compiler_params=pltpu.CompilerParams(vmem_limit_bytes=limit),
        name=name,
    )(*args)


def local(
    factors, feat_factor, feat_degree, coefficients, set_of_trade, party_of_set, threshold, weight
):
    n_trade, n_scen = lax.axis_size("trade"), lax.axis_size("scen")
    scen, nfac = factors.shape
    width, cols = coefficients.shape
    sets = cols // SET_SIZE
    lines = width // BLOCK
    own, chunk, grid = width // n_trade, width // n_scen, MAXDEG * nfac
    struct, vmem, dma = jax.ShapeDtypeStruct, pltpu.VMEM, pltpu.SemaphoreType.DMA
    i32 = jnp.int32
    outs = call(
        functools.partial(first_kernel, n_trade),
        [vmem((own, sets), f32)] * n_trade
        + [vmem((scen + INFO, sets), f32), vmem((nfac, scen), f32), vmem((lines, BLOCK), i32)]
        + [vmem((INFO, sets), f32), vmem((sets, cols), bf16)],
        [HBM] * 8,
        [
            factors.T,
            feat_factor.reshape(lines, BLOCK),
            feat_degree.reshape(lines, BLOCK),
            coefficients,
            set_of_trade.reshape(1, cols),
            party_of_set.reshape(1, sets),
            threshold.reshape(n_trade, sets),
            weight.reshape(n_trade, sets),
        ],
        "first",
        [
            vmem((nfac, scen), f32),
            vmem((lines, BLOCK), i32),
            vmem((lines, BLOCK), i32),
            vmem((1, cols), i32),
            vmem((1, sets), i32),
            vmem((n_trade, sets), f32),
            vmem((n_trade, sets), f32),
            vmem((lines, BLOCK, cols), f32),
            dma((7,)),
            dma((lines,)),
        ],
        limit=32 << 20,
    )
    folded, (expo, fact, key, side, member) = outs[:n_trade], outs[n_trade:]
    everything = lax.all_gather(expo, "trade", axis=0, tiled=True)
    (msg,) = call(
        functools.partial(second_kernel, n_trade),
        [vmem((scen + INFO + nfac * scen // sets, sets), f32)],
        [VMEM] * 3,
        [everything, side, fact],
        "second",
        limit=8 << 20,
    )
    peer = lax.ppermute(msg, "scen", [(i, i ^ 1) for i in range(n_scen)])
    half, chosen = call(
        functools.partial(middle_kernel, n_scen, nfac, scen),
        [vmem((grid, sets), f32), vmem((width // 2, grid), bf16)],
        [VMEM] * 2,
        [msg, key],
        "middle",
        [vmem((width, BLOCK), f32)],
        limit=8 << 20,
    )
    msg, *later = lax.optimization_barrier((msg, *folded[1:]))
    moved = [folded[0]] + [
        lax.ppermute(later[k - 1], "trade", [(i, i ^ k) for i in range(n_trade)])
        for k in range(1, n_trade)
    ]
    chunks = call(
        functools.partial(third_kernel, n_scen, nfac, scen),
        [vmem((chunk + INFO, sets), f32)] * (n_scen // 2),
        [VMEM] * 4,
        [peer, msg, half, chosen],
        "third",
        limit=8 << 20,
    )
    chunks = [chunks[0]] + [
        lax.ppermute(chunks[j], "scen", [(i, i ^ (2 * j)) for i in range(n_scen)])
        for j in [*range(n_scen // 4, n_scen // 2), *range(1, n_scen // 4)]
    ]
    (feature_sens,) = call(
        functools.partial(feature_kernel, n_trade),
        [struct((own, scen), f32)],
        [VMEM] * (n_trade + 1),
        [everything, *moved],
        "feature",
        [vmem((own, scen), f32), dma],
        flops=2 * 10**9,
        limit=8 << 20,
    )
    xva, coef_sens = call(
        functools.partial(last_kernel, n_scen // 2, 1.0 / (scen * n_scen)),
        [struct((1, sets), f32), struct((chunk, cols), f32)],
        [VMEM] * (n_scen // 2 + 1),
        [member, *chunks],
        "last",
        [vmem((1, sets), f32), vmem((chunk, cols), f32), dma((5,))],
        limit=8 << 20,
    )
    return (xva.reshape(sets), coef_sens, feature_sens)


def solution(mesh):
    in_specs = (P("scen", None), P(), P(), P(None, "trade"), P("trade"), P("trade"), P(), P())
    out_specs = (P("trade"), P("scen", "trade"), P("trade", "scen"))
    return jax.shard_map(local, mesh=mesh, in_specs=in_specs, out_specs=out_specs, check_vma=False)
```

```python
import functools

import jax
import jax.numpy as jnp
from jax import lax
from jax.experimental import pallas as pl
from jax.experimental.pallas import tpu as pltpu
from jax.sharding import PartitionSpec as P


MAXDEG = 12
SET_SIZE = 16
INFO = 8
BLOCK = 128

f32 = jnp.float32
bf16 = jnp.bfloat16
VMEM = pl.BlockSpec(memory_space=pltpu.VMEM)
HBM = pl.BlockSpec(memory_space=pltpu.HBM)


def split(value):
    high = value.astype(bf16)
    low = (value - high.astype(f32)).astype(bf16)
    return high, low


def nn(left, right):
    return lax.dot_general(left, right, (((1,), (0,)), ((), ())), preferred_element_type=f32)


def nt(left, right):
    return lax.dot_general(left, right, (((1,), (1,)), ((), ())), preferred_element_type=f32)


def pair_nn(left, right):
    cols = right[0].shape[1]
    both = nn(left[0], jnp.concatenate(right, axis=1))
    return both[:, :cols] + both[:, cols:] + nn(left[1], right[0])


def iota(shape, dim):
    return lax.broadcasted_iota(jnp.int32, shape, dim)


def column(row):
    n = row.shape[1]
    return jnp.transpose(jnp.broadcast_to(row.astype(f32), (n, n)))


def one_hot(test):
    return jnp.where(test, f32(1), f32(0)).astype(bf16)


def pick(table, ids):
    rows, lanes = table.shape
    total = jnp.zeros((1, ids.shape[1]), f32)
    for r in range(rows):
        here = column(table[r : r + 1, :])
        where = iota((lanes, ids.shape[1]), 0) + r * lanes == ids
        total = total + jnp.sum(jnp.where(where, here[:, : ids.shape[1]], 0.0), axis=0, keepdims=True)
    return total


def basis(points):
    before, current = jnp.ones_like(points), points
    rows = [current]
    for _ in range(2, MAXDEG + 1):
        before, current = current, 2.0 * points * current - before
        rows.append(current)
    return jnp.concatenate(rows, axis=0)


def first_kernel(n_trade, *refs):
    ins, rest = refs[:8], refs[8:]
    folded_refs, rest = rest[:n_trade], rest[n_trade:]
    expo_ref, fact_out, key_out, side_out, member_out = rest[:5]
    fact_ref, factor_ref, degree_ref, set_ref, party_ref, thr_ref, wgt_ref, coef_buf, small, sems = rest[5:]
    fact_hbm, factor_hbm, degree_hbm, coef_hbm, set_hbm, party_hbm, thr_hbm, wgt_hbm = ins
    me = lax.axis_index("trade")
    width, cols = coef_hbm.shape
    sets = cols // SET_SIZE
    nfac, scen = fact_ref.shape
    own = width // n_trade
    steps = width // BLOCK
    per = own // BLOCK

    loads = [
        pltpu.make_async_copy(source, target, small.at[i])
        for i, (source, target) in enumerate(
            [
                (fact_hbm, fact_ref),
                (set_hbm, set_ref),
                (factor_hbm, factor_ref),
                (degree_hbm, degree_ref),
                (party_hbm, party_ref),
                (thr_hbm, thr_ref),
                (wgt_hbm, wgt_ref),
            ]
        )
    ]

    def start_row(step):
        return pl.multiple_of((me ^ (step // per)) * own + (step % per) * BLOCK, BLOCK)

    def copy(step):
        return pltpu.make_async_copy(
            coef_hbm.at[pl.ds(start_row(step), BLOCK), :], coef_buf.at[step], sems.at[step]
        )

    for load in loads:
        load.start()
    for step in range(steps):
        copy(step).start(priority=1)
    for load in loads:
        load.wait()
    member = jnp.where(set_ref[...] - me * sets == iota((sets, cols), 0), f32(1), f32(0))
    member_out[...] = member.astype(bf16)
    turned_member = jnp.transpose(member).astype(bf16)
    fact_out[...] = fact_ref[...]
    table = split(jnp.transpose(basis(fact_ref[...])))
    key_out[...] = factor_ref[...] + nfac * (degree_ref[...] - 1)
    party = party_ref[...]
    thr_row = pick(thr_ref[...], party)
    wgt_row = pick(wgt_ref[...], party)
    line = iota((INFO, sets), 0)
    expo_ref[scen:, :] = jnp.where(line == 0, party.astype(f32), jnp.where(line == 1, thr_row, wgt_row))
    side_out[...] = jnp.where(line == 0, thr_ref[pl.ds(me, 1), :], wgt_ref[pl.ds(me, 1), :])
    keys = [key_out[pl.ds(lax.div(start_row(step), BLOCK), 1), :] for step in range(steps)]
    chosen = one_hot(iota((MAXDEG * nfac, width), 0) == jnp.concatenate(keys, axis=1))
    phi = [nn(part, chosen).astype(bf16) for part in table]
    done, total = 0, None
    for size in (steps // 2, steps - steps // 2):
        group = range(done, done + size)
        for step in group:
            copy(step).wait()
        highs, lows = [], []
        for step in group:
            coef_high, coef_low = split(coef_buf[step])
            folded = nn(coef_high, turned_member) + nn(coef_low, turned_member)
            folded_refs[step // per][pl.ds((step % per) * BLOCK, BLOCK), :] = folded
            high, low = split(folded)
            highs.append(high)
            lows.append(low)
        here = slice(done * BLOCK, (done + size) * BLOCK)
        part = pair_nn(
            [piece[:, here] for piece in phi],
            [jnp.concatenate(highs, axis=0), jnp.concatenate(lows, axis=0)],
        )
        total = part if total is None else total + part
        done += size
    expo_ref[:scen, :] = total


def blocks_of(refs):
    scen = refs[0].shape[0] - INFO
    expo = [split(ref[:scen, :]) for ref in refs]
    pieces = [jnp.concatenate([e[i] for e in expo], axis=1) for i in range(2)]
    return pieces, [column(ref[scen : scen + 1, :]) for ref in refs]


def same_as(columns, row):
    return one_hot(jnp.concatenate([here == row for here in columns], axis=0))


def info_of(ref):
    info = ref[ref.shape[0] - INFO :, :]
    return info[0:1, :], info[1:2, :], info[2:3, :]


def second_kernel(n_trade, *refs):
    blocks, (side_ref, _, msg_ref) = refs[:n_trade], refs[n_trade:]
    trade = lax.axis_index("trade")
    scen, sets = blocks[0].shape[0] - INFO, blocks[0].shape[1]
    (high, low), columns = blocks_of(blocks)
    party, thr, wgt = info_of(blocks[0])
    mine = (iota((1, sets), 1) + trade * sets).astype(f32)
    right = jnp.concatenate([same_as(columns, party), same_as(columns, mine)], axis=1)
    netted = nn(high, right) + nn(low, right)
    msg_ref[:scen, :] = wgt * jax.nn.sigmoid(netted[:, :sets] - thr)
    soft = jax.nn.softplus(netted[:, sets:] - side_ref[0:1, :])
    msg_ref[scen:, :] = jnp.broadcast_to(
        jnp.sum(soft, axis=0, keepdims=True) * side_ref[1:2, :], (INFO, sets)
    )


def response(table, msg_ref):
    return pair_nn(table, split(msg_ref[: msg_ref.shape[0] - INFO, :]))


def middle_kernel(n_scen, msg_ref, fact_ref, peer_ref, key_ref, grid_ref, chosen_ref, high_ref, low_ref, column_ref):
    me = lax.axis_index("scen")
    lines = key_ref.shape[0]
    chunk = lines * BLOCK // n_scen
    for i in range(lines):
        column_ref[i * BLOCK : (i + 1) * BLOCK, :] = column(key_ref[i : i + 1, :])
    rows = grid_ref.shape[0]
    for j in range(n_scen // 2):
        here = column_ref[pl.ds(pl.multiple_of((me ^ (2 * j)) * chunk, chunk), chunk), :].astype(jnp.int32)
        for i in range(rows // BLOCK):
            chosen_ref[j * chunk : (j + 1) * chunk, i * BLOCK : (i + 1) * BLOCK] = one_hot(
                here == iota(here.shape, 1) + i * BLOCK
            )
    grid_ref[...] = response(split(basis(fact_ref[...])), msg_ref)
    high_ref[...], low_ref[...] = split(basis(peer_ref[...]))


def third_kernel(msg_ref, high_ref, low_ref, own_ref, grid_ref, chosen_ref, *chunk_refs):
    chunk = chosen_ref.shape[0] // len(chunk_refs)
    both = jnp.concatenate(split(grid_ref[...] + response((high_ref[...], low_ref[...]), msg_ref)), axis=1)
    scen, sets = msg_ref.shape[0] - INFO, msg_ref.shape[1]
    xva = msg_ref[scen:, :] + own_ref[scen:, :]
    for j, ref in enumerate(chunk_refs):
        part = nn(chosen_ref[j * chunk : (j + 1) * chunk, :], both)
        ref[:chunk, :] = part[:, :sets] + part[:, sets:]
        ref[chunk:, :] = xva


def feature_kernel(n_trade, *refs):
    blocks, folded_refs, (out_hbm, out_ref, sem) = refs[:n_trade], refs[n_trade : 2 * n_trade], refs[2 * n_trade :]
    (high, low), columns = blocks_of(blocks)
    total = jnp.zeros(out_ref.shape, f32)
    for k in range(n_trade):
        party, thr, wgt = info_of(blocks[k])
        same = same_as(columns, party)
        netted = nn(high, same) + nn(low, same)
        adj_high, adj_low = split(wgt * jax.nn.sigmoid(netted - thr))
        fold_high, fold_low = split(folded_refs[k][...])
        total = total + nt(fold_high, adj_high) + nt(fold_low, adj_high) + nt(fold_high, adj_low)
    out_ref[...] = total
    copy = pltpu.make_async_copy(out_ref, out_hbm, sem)
    copy.start()
    copy.wait()


def last_kernel(n_chunks, scale, member_ref, *refs):
    chunk_refs, (xva_hbm, out_hbm, xva_ref, out_ref, sems) = refs[:n_chunks], refs[n_chunks:]
    rows, cols = out_hbm.shape
    total = chunk_refs[0][...]
    for ref in chunk_refs[1:]:
        total = total + ref[...]
    total = total * scale
    xva_ref[...] = total[rows : rows + 1, :]
    first = pltpu.make_async_copy(xva_ref, xva_hbm, sems.at[0])
    first.start()
    high, low = split(total[:rows, :])
    copies = [first]
    pieces = sems.shape[0] - 1
    wide = cols // pieces
    for i in range(pieces):
        part = member_ref[:, i * wide : (i + 1) * wide]
        out_ref[:, i * wide : (i + 1) * wide] = nn(high, part) + nn(low, part)
        copies.append(
            pltpu.make_async_copy(
                out_ref.at[:, pl.ds(i * wide, wide)], out_hbm.at[:, pl.ds(i * wide, wide)], sems.at[i + 1]
            )
        )
        copies[-1].start()
    for copy in copies:
        copy.wait()


def call(kernel, out_shape, in_specs, args, scratch=(), flops=5 * 10**8, limit=None):
    args = [
        pltpu.with_memory_space_constraint(arg, pltpu.VMEM if spec is VMEM else pltpu.HBM)
        for arg, spec in zip(args, in_specs)
    ]
    specs = [HBM if isinstance(shape, jax.ShapeDtypeStruct) else VMEM for shape in out_shape]
    return pl.pallas_call(
        kernel,
        out_shape=out_shape,
        in_specs=in_specs,
        out_specs=specs,
        scratch_shapes=scratch,
        cost_estimate=pl.CostEstimate(flops=flops, bytes_accessed=10**5, transcendentals=0),
        compiler_params=pltpu.CompilerParams(vmem_limit_bytes=limit),
    )(*args)


def send(value, axis, k):
    return lax.ppermute(value, axis, [(i, i ^ k) for i in range(lax.axis_size(axis))])


def local(
    factors, feat_factor, feat_degree, coefficients, set_of_trade, party_of_set, threshold, weight
):
    n_trade, n_scen = lax.axis_size("trade"), lax.axis_size("scen")
    scen, nfac = factors.shape
    width, cols = coefficients.shape
    sets = cols // SET_SIZE
    lines = width // BLOCK
    own, chunk, grid = width // n_trade, width // n_scen, MAXDEG * nfac
    struct, vmem, dma = jax.ShapeDtypeStruct, pltpu.VMEM, pltpu.SemaphoreType.DMA
    i32 = jnp.int32
    outs = call(
        functools.partial(first_kernel, n_trade),
        [vmem((own, sets), f32)] * n_trade
        + [vmem((scen + INFO, sets), f32), vmem((nfac, scen), f32), vmem((lines, BLOCK), i32)]
        + [vmem((INFO, sets), f32), vmem((sets, cols), bf16)],
        [HBM] * 8,
        [
            factors.T,
            feat_factor.reshape(lines, BLOCK),
            feat_degree.reshape(lines, BLOCK),
            coefficients,
            set_of_trade.reshape(1, cols),
            party_of_set.reshape(1, sets),
            threshold.reshape(n_trade, sets),
            weight.reshape(n_trade, sets),
        ],
        [
            vmem((nfac, scen), f32),
            vmem((lines, BLOCK), i32),
            vmem((lines, BLOCK), i32),
            vmem((1, cols), i32),
            vmem((1, sets), i32),
            vmem((n_trade, sets), f32),
            vmem((n_trade, sets), f32),
            vmem((lines, BLOCK, cols), f32),
            dma((7,)),
            dma((lines,)),
        ],
        limit=32 << 20,
    )
    folded, (expo, fact, key, side, member) = outs[:n_trade], outs[n_trade:]
    blocks = [expo] + [None] * (n_trade - 1)
    for k in range(2, n_trade, 2):
        blocks[k] = send(expo, "trade", k)
    blocks[1] = send(expo, "trade", 1)
    for k in range(2, n_trade, 2):
        blocks[k + 1] = send(blocks[k], "trade", 1)
    peer_fact = send(fact, "scen", 1)
    (msg,) = call(
        functools.partial(second_kernel, n_trade),
        [vmem((scen + INFO, sets), f32)],
        [VMEM] * (n_trade + 2),
        [*blocks, side, peer_fact],
        limit=8 << 20,
    )
    peer = send(msg, "scen", 1)
    half, chosen, *peer_table = call(
        functools.partial(middle_kernel, n_scen),
        [vmem((grid, sets), f32), vmem((width // 2, grid), bf16)] + [vmem((grid, scen), bf16)] * 2,
        [VMEM] * 4,
        [msg, fact, peer_fact, key],
        [vmem((width, BLOCK), f32)],
        limit=8 << 20,
    )
    msg, *later = lax.optimization_barrier((msg, *folded[1:]))
    moved = [folded[0]] + [send(later[k - 1], "trade", k) for k in range(1, n_trade)]
    chunks = call(
        third_kernel,
        [vmem((chunk + INFO, sets), f32)] * (n_scen // 2),
        [VMEM] * 6,
        [peer, *peer_table, msg, half, chosen],
        limit=8 << 20,
    )
    chunks = [chunks[0]] + [
        send(chunks[j], "scen", 2 * j)
        for j in [*range(n_scen // 4, n_scen // 2), *range(1, n_scen // 4)]
    ]
    (feature_sens,) = call(
        functools.partial(feature_kernel, n_trade),
        [struct((own, scen), f32)],
        [VMEM] * (2 * n_trade),
        [*blocks, *moved],
        [vmem((own, scen), f32), dma],
        flops=2 * 10**9,
        limit=8 << 20,
    )
    xva, coef_sens = call(
        functools.partial(last_kernel, n_scen // 2, 1.0 / (scen * n_scen)),
        [struct((1, sets), f32), struct((chunk, cols), f32)],
        [VMEM] * (n_scen // 2 + 1),
        [member, *chunks],
        [vmem((1, sets), f32), vmem((chunk, cols), f32), dma((5,))],
        limit=8 << 20,
    )
    return (xva.reshape(sets), coef_sens, feature_sens)


def solution(mesh):
    in_specs = (P("scen", None), P(), P(), P(None, "trade"), P("trade"), P("trade"), P(), P())
    out_specs = (P("trade"), P("scen", "trade"), P("trade", "scen"))
    return jax.shard_map(local, mesh=mesh, in_specs=in_specs, out_specs=out_specs, check_vma=False)
```

```python
import functools

import jax
import jax.numpy as jnp
from jax import lax
from jax.experimental import pallas as pl
from jax.experimental.pallas import tpu as pltpu
from jax.sharding import PartitionSpec as P


MAXDEG = 12
SET_SIZE = 16
INFO = 8
BLOCK = 128

f32 = jnp.float32
bf16 = jnp.bfloat16
VMEM = pl.BlockSpec(memory_space=pltpu.VMEM)
HBM = pl.BlockSpec(memory_space=pltpu.HBM)


def split(value):
    high = value.astype(bf16)
    low = (value - high.astype(f32)).astype(bf16)
    return high, low


def nn(left, right):
    return lax.dot_general(left, right, (((1,), (0,)), ((), ())), preferred_element_type=f32)


def nt(left, right):
    return lax.dot_general(left, right, (((1,), (1,)), ((), ())), preferred_element_type=f32)


def pair_nn(left, right):
    cols = right[0].shape[1]
    both = nn(left[0], jnp.concatenate(right, axis=1))
    return both[:, :cols] + both[:, cols:] + nn(left[1], right[0])


def iota(shape, dim):
    return lax.broadcasted_iota(jnp.int32, shape, dim)


def column(row):
    n = row.shape[1]
    return jnp.transpose(jnp.broadcast_to(row.astype(f32), (n, n)))


def one_hot(test):
    return jnp.where(test, f32(1), f32(0)).astype(bf16)


def pick(table, ids):
    rows, lanes = table.shape
    total = jnp.zeros((1, ids.shape[1]), f32)
    for r in range(rows):
        here = column(table[r : r + 1, :])
        where = iota((lanes, ids.shape[1]), 0) + r * lanes == ids
        total = total + jnp.sum(jnp.where(where, here[:, : ids.shape[1]], 0.0), axis=0, keepdims=True)
    return total


def basis(points):
    before, current = jnp.ones_like(points), points
    rows = [current]
    for _ in range(2, MAXDEG + 1):
        before, current = current, 2.0 * points * current - before
        rows.append(current)
    return jnp.concatenate(rows, axis=0)


def first_kernel(n_trade, *refs):
    ins, rest = refs[:8], refs[8:]
    folded_refs, rest = rest[:n_trade], rest[n_trade:]
    expo_ref, fact_out, key_out, side_out, member_out = rest[:5]
    fact_ref, factor_ref, degree_ref, set_ref, party_ref, thr_ref, wgt_ref, coef_buf, small, sems = rest[5:]
    fact_hbm, factor_hbm, degree_hbm, coef_hbm, set_hbm, party_hbm, thr_hbm, wgt_hbm = ins
    me = lax.axis_index("trade")
    width, cols = coef_hbm.shape
    sets = cols // SET_SIZE
    nfac, scen = fact_ref.shape
    own = width // n_trade
    steps = width // BLOCK
    per = own // BLOCK

    loads = [
        pltpu.make_async_copy(source, target, small.at[i])
        for i, (source, target) in enumerate(
            [
                (fact_hbm, fact_ref),
                (set_hbm, set_ref),
                (factor_hbm, factor_ref),
                (degree_hbm, degree_ref),
                (party_hbm, party_ref),
                (thr_hbm, thr_ref),
                (wgt_hbm, wgt_ref),
            ]
        )
    ]

    def start_row(step):
        return pl.multiple_of((me ^ (step // per)) * own + (step % per) * BLOCK, BLOCK)

    def copy(step):
        return pltpu.make_async_copy(
            coef_hbm.at[pl.ds(start_row(step), BLOCK), :], coef_buf.at[step], sems.at[step]
        )

    for load in loads:
        load.start()
    for step in range(steps):
        copy(step).start(priority=1)
    for load in loads:
        load.wait()
    member = jnp.where(set_ref[...] - me * sets == iota((sets, cols), 0), f32(1), f32(0))
    member_out[...] = member.astype(bf16)
    turned_member = jnp.transpose(member).astype(bf16)
    fact_out[...] = fact_ref[...]
    table = split(jnp.transpose(basis(fact_ref[...])))
    key_out[...] = factor_ref[...] + nfac * (degree_ref[...] - 1)
    party = party_ref[...]
    thr_row = pick(thr_ref[...], party)
    wgt_row = pick(wgt_ref[...], party)
    line = iota((INFO, sets), 0)
    expo_ref[scen:, :] = jnp.where(line == 0, party.astype(f32), jnp.where(line == 1, thr_row, wgt_row))
    side_out[...] = jnp.where(line == 0, thr_ref[pl.ds(me, 1), :], wgt_ref[pl.ds(me, 1), :])
    keys = [key_out[pl.ds(lax.div(start_row(step), BLOCK), 1), :] for step in range(steps)]
    chosen = one_hot(iota((MAXDEG * nfac, width), 0) == jnp.concatenate(keys, axis=1))
    phi = [nn(part, chosen).astype(bf16) for part in table]
    done, total = 0, None
    for size in (steps // 2, steps - steps // 2):
        group = range(done, done + size)
        for step in group:
            copy(step).wait()
        highs, lows = [], []
        for step in group:
            coef_high, coef_low = split(coef_buf[step])
            both = nn(jnp.concatenate([coef_high, coef_low], axis=0), turned_member)
            folded = both[:BLOCK] + both[BLOCK:]
            folded_refs[step // per][pl.ds((step % per) * BLOCK, BLOCK), :] = folded
            high, low = split(folded)
            highs.append(high)
            lows.append(low)
        here = slice(done * BLOCK, (done + size) * BLOCK)
        part = pair_nn(
            [piece[:, here] for piece in phi],
            [jnp.concatenate(highs, axis=0), jnp.concatenate(lows, axis=0)],
        )
        total = part if total is None else total + part
        done += size
    expo_ref[:scen, :] = total


def blocks_of(refs):
    scen = refs[0].shape[0] - INFO
    expo = [split(ref[:scen, :]) for ref in refs]
    pieces = [jnp.concatenate([e[i] for e in expo], axis=1) for i in range(2)]
    return pieces, [column(ref[scen : scen + 1, :]) for ref in refs]


def same_as(columns, row):
    return one_hot(jnp.concatenate([here == row for here in columns], axis=0))


def info_of(ref):
    info = ref[ref.shape[0] - INFO :, :]
    return info[0:1, :], info[1:2, :], info[2:3, :]


def net_kernel(n_blocks, *refs):
    blocks, own_ref, *total, out_ref = refs[:n_blocks], *refs[n_blocks:]
    trade = lax.axis_index("trade")
    sets = own_ref.shape[1]
    (high, low), columns = blocks_of(blocks)
    party, _, _ = info_of(own_ref)
    mine = (iota((1, sets), 1) + trade * sets).astype(f32)
    right = jnp.concatenate([same_as(columns, party), same_as(columns, mine)], axis=1)
    netted = nn(high, right) + nn(low, right)
    out_ref[...] = total[0][...] + netted if total else netted


def second_kernel(n_blocks, *refs):
    *ins, side_ref, _, msg_ref, net_ref = refs
    net_kernel(n_blocks, *ins, net_ref)
    own_ref = ins[n_blocks]
    scen, sets = own_ref.shape[0] - INFO, own_ref.shape[1]
    _, thr, wgt = info_of(own_ref)
    msg_ref[:scen, :] = wgt * jax.nn.sigmoid(net_ref[:, :sets] - thr)
    soft = jax.nn.softplus(net_ref[:, sets:] - side_ref[0:1, :])
    msg_ref[scen:, :] = jnp.broadcast_to(
        jnp.sum(soft, axis=0, keepdims=True) * side_ref[1:2, :], (INFO, sets)
    )


def choose_kernel(n_scen, key_ref, chosen_ref, column_ref):
    me = lax.axis_index("scen")
    lines = key_ref.shape[0]
    chunk = lines * BLOCK // n_scen
    for i in range(lines):
        column_ref[i * BLOCK : (i + 1) * BLOCK, :] = column(key_ref[i : i + 1, :])
    for j in range(n_scen // 2):
        here = column_ref[pl.ds(pl.multiple_of((me ^ (2 * j)) * chunk, chunk), chunk), :].astype(jnp.int32)
        for i in range(chosen_ref.shape[1] // BLOCK):
            chosen_ref[j * chunk : (j + 1) * chunk, i * BLOCK : (i + 1) * BLOCK] = one_hot(
                here == iota(here.shape, 1) + i * BLOCK
            )


def middle_kernel(msg_ref, fact_ref, peer_ref, chosen_ref, part_ref, high_ref, low_ref):
    adj = split(msg_ref[: msg_ref.shape[0] - INFO, :])
    sets = msg_ref.shape[1]
    chosen = chosen_ref[...]
    grid = pair_nn(split(basis(fact_ref[...])), adj)
    part = nn(chosen, jnp.concatenate(split(grid), axis=1))
    part_ref[...] = part[:, :sets] + part[:, sets:]
    high, low = split(basis(peer_ref[...]))
    high_ref[...] = nn(chosen, high).astype(bf16)
    low_ref[...] = nn(chosen, low).astype(bf16)


def third_kernel(msg_ref, own_ref, part_ref, high_ref, low_ref, *chunk_refs):
    chunk = part_ref.shape[0] // len(chunk_refs)
    scen = msg_ref.shape[0] - INFO
    adj = split(msg_ref[:scen, :])
    xva = msg_ref[scen:, :] + own_ref[scen:, :]
    for j, ref in enumerate(chunk_refs):
        rows = slice(j * chunk, (j + 1) * chunk)
        ref[:chunk, :] = part_ref[rows, :] + pair_nn((high_ref[rows, :], low_ref[rows, :]), adj)
        ref[chunk:, :] = xva


def feature_kernel(n_trade, *refs):
    blocks, folded_refs, (out_hbm, out_ref, sem) = refs[:n_trade], refs[n_trade : 2 * n_trade], refs[2 * n_trade :]
    (high, low), columns = blocks_of(blocks)
    total = jnp.zeros(out_ref.shape, f32)
    for k in range(n_trade):
        party, thr, wgt = info_of(blocks[k])
        same = same_as(columns, party)
        netted = nn(high, same) + nn(low, same)
        adj_high, adj_low = split(wgt * jax.nn.sigmoid(netted - thr))
        fold_high, fold_low = split(folded_refs[k][...])
        total = total + nt(fold_high, adj_high) + nt(fold_low, adj_high) + nt(fold_high, adj_low)
    out_ref[...] = total
    copy = pltpu.make_async_copy(out_ref, out_hbm, sem)
    copy.start()
    copy.wait()


def last_kernel(n_chunks, scale, member_ref, *refs):
    chunk_refs, (xva_hbm, out_hbm, xva_ref, out_ref, sems) = refs[:n_chunks], refs[n_chunks:]
    rows, cols = out_hbm.shape
    total = chunk_refs[0][...]
    for ref in chunk_refs[1:]:
        total = total + ref[...]
    total = total * scale
    xva_ref[...] = total[rows : rows + 1, :]
    first = pltpu.make_async_copy(xva_ref, xva_hbm, sems.at[0])
    first.start()
    high, low = split(total[:rows, :])
    copies = [first]
    pieces = sems.shape[0] - 1
    wide = cols // pieces
    for i in range(pieces):
        part = member_ref[:, i * wide : (i + 1) * wide]
        out_ref[:, i * wide : (i + 1) * wide] = nn(high, part) + nn(low, part)
        copies.append(
            pltpu.make_async_copy(
                out_ref.at[:, pl.ds(i * wide, wide)], out_hbm.at[:, pl.ds(i * wide, wide)], sems.at[i + 1]
            )
        )
        copies[-1].start()
    for copy in copies:
        copy.wait()


def call(kernel, out_shape, in_specs, args, scratch=(), flops=5 * 10**8, limit=None):
    args = [
        pltpu.with_memory_space_constraint(arg, pltpu.VMEM if spec is VMEM else pltpu.HBM)
        for arg, spec in zip(args, in_specs)
    ]
    specs = [HBM if isinstance(shape, jax.ShapeDtypeStruct) else VMEM for shape in out_shape]
    return pl.pallas_call(
        kernel,
        out_shape=out_shape,
        in_specs=in_specs,
        out_specs=specs,
        scratch_shapes=scratch,
        cost_estimate=pl.CostEstimate(flops=flops, bytes_accessed=10**5, transcendentals=0),
        compiler_params=pltpu.CompilerParams(vmem_limit_bytes=limit),
    )(*args)


def send(value, axis, k):
    return lax.ppermute(value, axis, [(i, i ^ k) for i in range(lax.axis_size(axis))])


def local(
    factors, feat_factor, feat_degree, coefficients, set_of_trade, party_of_set, threshold, weight
):
    n_trade, n_scen = lax.axis_size("trade"), lax.axis_size("scen")
    scen, nfac = factors.shape
    width, cols = coefficients.shape
    sets = cols // SET_SIZE
    lines = width // BLOCK
    own, chunk, grid = width // n_trade, width // n_scen, MAXDEG * nfac
    struct, vmem, dma = jax.ShapeDtypeStruct, pltpu.VMEM, pltpu.SemaphoreType.DMA
    i32 = jnp.int32
    outs = call(
        functools.partial(first_kernel, n_trade),
        [vmem((own, sets), f32)] * n_trade
        + [vmem((scen + INFO, sets), f32), vmem((nfac, scen), f32), vmem((lines, BLOCK), i32)]
        + [vmem((INFO, sets), f32), vmem((sets, cols), bf16)],
        [HBM] * 8,
        [
            factors.T,
            feat_factor.reshape(lines, BLOCK),
            feat_degree.reshape(lines, BLOCK),
            coefficients,
            set_of_trade.reshape(1, cols),
            party_of_set.reshape(1, sets),
            threshold.reshape(n_trade, sets),
            weight.reshape(n_trade, sets),
        ],
        [
            vmem((nfac, scen), f32),
            vmem((lines, BLOCK), i32),
            vmem((lines, BLOCK), i32),
            vmem((1, cols), i32),
            vmem((1, sets), i32),
            vmem((n_trade, sets), f32),
            vmem((n_trade, sets), f32),
            vmem((lines, BLOCK, cols), f32),
            dma((7,)),
            dma((lines,)),
        ],
        limit=32 << 20,
    )
    folded, (expo, fact, key, side, member) = outs[:n_trade], outs[n_trade:]
    blocks = [expo] + [None] * (n_trade - 1)
    for k in range(2, n_trade, 2):
        blocks[k] = send(expo, "trade", k)
    blocks[1] = send(expo, "trade", 1)
    for k in range(2, n_trade, 2):
        blocks[k + 1] = send(blocks[k], "trade", 1)
    peer_fact = send(fact, "scen", 1)
    (chosen,) = call(
        functools.partial(choose_kernel, n_scen),
        [vmem((width // 2, grid), bf16)],
        [VMEM],
        [key],
        [vmem((width, BLOCK), f32)],
        limit=8 << 20,
    )
    total = []
    for here in (blocks[:2], blocks[2::2]):
        total = call(
            functools.partial(net_kernel, len(here)),
            [vmem((scen, 2 * sets), f32)],
            [VMEM] * (len(here) + 1 + len(total)),
            [*here, expo, *total],
            limit=8 << 20,
        )
    here = blocks[3::2]
    (msg,) = call(
        functools.partial(second_kernel, len(here)),
        [vmem((scen + INFO, sets), f32)],
        [VMEM] * (len(here) + 4),
        [*here, expo, *total, side, peer_fact],
        [vmem((scen, 2 * sets), f32)],
        limit=8 << 20,
    )
    peer = send(msg, "scen", 1)
    middle = call(
        middle_kernel,
        [vmem((width // 2, sets), f32)] + [vmem((width // 2, scen), bf16)] * 2,
        [VMEM] * 4,
        [msg, fact, peer_fact, chosen],
        limit=8 << 20,
    )
    msg, *later = lax.optimization_barrier((msg, *folded[1:]))
    moved = [folded[0]] + [send(later[k - 1], "trade", k) for k in range(1, n_trade)]
    chunks = call(
        third_kernel,
        [vmem((chunk + INFO, sets), f32)] * (n_scen // 2),
        [VMEM] * 5,
        [peer, msg, *middle],
        limit=8 << 20,
    )
    chunks = [chunks[0]] + [
        send(chunks[j], "scen", 2 * j)
        for j in [*range(n_scen // 4, n_scen // 2), *range(1, n_scen // 4)]
    ]
    (feature_sens,) = call(
        functools.partial(feature_kernel, n_trade),
        [struct((own, scen), f32)],
        [VMEM] * (2 * n_trade),
        [*blocks, *moved],
        [vmem((own, scen), f32), dma],
        flops=2 * 10**9,
        limit=8 << 20,
    )
    xva, coef_sens = call(
        functools.partial(last_kernel, n_scen // 2, 1.0 / (scen * n_scen)),
        [struct((1, sets), f32), struct((chunk, cols), f32)],
        [VMEM] * (n_scen // 2 + 1),
        [member, *chunks],
        [vmem((1, sets), f32), vmem((chunk, cols), f32), dma((5,))],
        limit=8 << 20,
    )
    return (xva.reshape(sets), coef_sens, feature_sens)


def solution(mesh):
    in_specs = (P("scen", None), P(), P(), P(None, "trade"), P("trade"), P("trade"), P(), P())
    out_specs = (P("trade"), P("scen", "trade"), P("trade", "scen"))
    return jax.shard_map(local, mesh=mesh, in_specs=in_specs, out_specs=out_specs, check_vma=False)
```

```python
import functools

import jax
import jax.numpy as jnp
from jax import lax
from jax.experimental import pallas as pl
from jax.experimental.pallas import tpu as pltpu
from jax.sharding import PartitionSpec as P


MAXDEG = 12
SET_SIZE = 16
INFO = 8
BLOCK = 128

f32 = jnp.float32
bf16 = jnp.bfloat16
VMEM = pl.BlockSpec(memory_space=pltpu.VMEM)
HBM = pl.BlockSpec(memory_space=pltpu.HBM)


def split(value):
    high = value.astype(bf16)
    low = (value - high.astype(f32)).astype(bf16)
    return high, low


def nn(left, right):
    return lax.dot_general(left, right, (((1,), (0,)), ((), ())), preferred_element_type=f32)


def nt(left, right):
    return lax.dot_general(left, right, (((1,), (1,)), ((), ())), preferred_element_type=f32)


def pair_nn(left, right):
    cols = right[0].shape[1]
    both = nn(left[0], jnp.concatenate(right, axis=1))
    return both[:, :cols] + both[:, cols:] + nn(left[1], right[0])


def iota(shape, dim):
    return lax.broadcasted_iota(jnp.int32, shape, dim)


def column(row):
    n = row.shape[1]
    return jnp.transpose(jnp.broadcast_to(row.astype(f32), (n, n)))


def one_hot(test):
    return jnp.where(test, f32(1), f32(0)).astype(bf16)


def pick(table, ids):
    rows, lanes = table.shape
    total = jnp.zeros((1, ids.shape[1]), f32)
    for r in range(rows):
        here = column(table[r : r + 1, :])
        where = iota((lanes, ids.shape[1]), 0) + r * lanes == ids
        total = total + jnp.sum(jnp.where(where, here[:, : ids.shape[1]], 0.0), axis=0, keepdims=True)
    return total


def basis(points):
    before, current = jnp.ones_like(points), points
    rows = [current]
    for _ in range(2, MAXDEG + 1):
        before, current = current, 2.0 * points * current - before
        rows.append(current)
    return jnp.concatenate(rows, axis=0)


def first_kernel(n_trade, *refs):
    ins, rest = refs[:8], refs[8:]
    folded_refs, rest = rest[:n_trade], rest[n_trade:]
    expo_ref, fact_out, key_out, side_out, member_out = rest[:5]
    fact_ref, factor_ref, degree_ref, set_ref, party_ref, thr_ref, wgt_ref, coef_buf, small, sems = rest[5:]
    fact_hbm, factor_hbm, degree_hbm, coef_hbm, set_hbm, party_hbm, thr_hbm, wgt_hbm = ins
    me = lax.axis_index("trade")
    width, cols = coef_hbm.shape
    sets = cols // SET_SIZE
    nfac, scen = fact_ref.shape
    own = width // n_trade
    steps = width // BLOCK
    per = own // BLOCK

    loads = [
        pltpu.make_async_copy(source, target, small.at[i])
        for i, (source, target) in enumerate(
            [
                (fact_hbm, fact_ref),
                (set_hbm, set_ref),
                (factor_hbm, factor_ref),
                (degree_hbm, degree_ref),
                (party_hbm, party_ref),
                (thr_hbm, thr_ref),
                (wgt_hbm, wgt_ref),
            ]
        )
    ]

    def start_row(step):
        return pl.multiple_of((me ^ (step // per)) * own + (step % per) * BLOCK, BLOCK)

    def copy(step):
        return pltpu.make_async_copy(
            coef_hbm.at[pl.ds(start_row(step), BLOCK), :], coef_buf.at[step], sems.at[step]
        )

    for load in loads:
        load.start()
    for step in range(steps):
        copy(step).start(priority=1)
    for load in loads:
        load.wait()
    member = jnp.where(set_ref[...] - me * sets == iota((sets, cols), 0), f32(1), f32(0))
    member_out[...] = member.astype(bf16)
    turned_member = jnp.transpose(member).astype(bf16)
    fact_out[...] = fact_ref[...]
    table = split(jnp.transpose(basis(fact_ref[...])))
    key_out[...] = factor_ref[...] + nfac * (degree_ref[...] - 1)
    party = party_ref[...]
    thr_row = pick(thr_ref[...], party)
    wgt_row = pick(wgt_ref[...], party)
    line = iota((INFO, sets), 0)
    expo_ref[scen:, :] = jnp.where(line == 0, party.astype(f32), jnp.where(line == 1, thr_row, wgt_row))
    side_out[...] = jnp.where(line == 0, thr_ref[pl.ds(me, 1), :], wgt_ref[pl.ds(me, 1), :])
    keys = [key_out[pl.ds(lax.div(start_row(step), BLOCK), 1), :] for step in range(steps)]
    chosen = one_hot(iota((MAXDEG * nfac, width), 0) == jnp.concatenate(keys, axis=1))
    phi = [nn(part, chosen).astype(bf16) for part in table]
    done, total = 0, None
    for size in (steps // 2, steps - steps // 2):
        group = range(done, done + size)
        for step in group:
            copy(step).wait()
        highs, lows = [], []
        for step in group:
            coef_high, coef_low = split(coef_buf[step])
            both = nn(jnp.concatenate([coef_high, coef_low], axis=0), turned_member)
            folded = both[:BLOCK] + both[BLOCK:]
            folded_refs[step // per][pl.ds((step % per) * BLOCK, BLOCK), :] = folded
            high, low = split(folded)
            highs.append(high)
            lows.append(low)
        here = slice(done * BLOCK, (done + size) * BLOCK)
        part = pair_nn(
            [piece[:, here] for piece in phi],
            [jnp.concatenate(highs, axis=0), jnp.concatenate(lows, axis=0)],
        )
        total = part if total is None else total + part
        done += size
    expo_ref[:scen, :] = total


def blocks_of(refs):
    scen = refs[0].shape[0] - INFO
    expo = [split(ref[:scen, :]) for ref in refs]
    pieces = [jnp.concatenate([e[i] for e in expo], axis=1) for i in range(2)]
    return pieces, [column(ref[scen : scen + 1, :]) for ref in refs]


def same_as(columns, row):
    return one_hot(jnp.concatenate([here == row for here in columns], axis=0))


def info_of(ref):
    info = ref[ref.shape[0] - INFO :, :]
    return info[0:1, :], info[1:2, :], info[2:3, :]


def net_kernel(n_blocks, *refs):
    blocks, own_ref, *total, out_ref = refs[:n_blocks], *refs[n_blocks:]
    trade = lax.axis_index("trade")
    sets = own_ref.shape[1]
    (high, low), columns = blocks_of(blocks)
    party, _, _ = info_of(own_ref)
    mine = (iota((1, sets), 1) + trade * sets).astype(f32)
    right = jnp.concatenate([same_as(columns, party), same_as(columns, mine)], axis=1)
    netted = nn(high, right) + nn(low, right)
    out_ref[...] = total[0][...] + netted if total else netted


def second_kernel(n_blocks, *refs):
    *ins, side_ref, _, msg_ref, net_ref = refs
    net_kernel(n_blocks, *ins, net_ref)
    own_ref = ins[n_blocks]
    scen, sets = own_ref.shape[0] - INFO, own_ref.shape[1]
    _, thr, wgt = info_of(own_ref)
    msg_ref[:scen, :] = wgt * jax.nn.sigmoid(net_ref[:, :sets] - thr)
    soft = jax.nn.softplus(net_ref[:, sets:] - side_ref[0:1, :])
    msg_ref[scen:, :] = jnp.broadcast_to(
        jnp.sum(soft, axis=0, keepdims=True) * side_ref[1:2, :], (INFO, sets)
    )


def choose_kernel(n_scen, key_ref, chosen_ref, column_ref):
    me = lax.axis_index("scen")
    lines = key_ref.shape[0]
    chunk = lines * BLOCK // n_scen
    for i in range(lines):
        column_ref[i * BLOCK : (i + 1) * BLOCK, :] = column(key_ref[i : i + 1, :])
    for j in range(n_scen // 2):
        here = column_ref[pl.ds(pl.multiple_of((me ^ (2 * j)) * chunk, chunk), chunk), :].astype(jnp.int32)
        for i in range(chosen_ref.shape[1] // BLOCK):
            chosen_ref[j * chunk : (j + 1) * chunk, i * BLOCK : (i + 1) * BLOCK] = one_hot(
                here == iota(here.shape, 1) + i * BLOCK
            )


def middle_kernel(msg_ref, fact_ref, peer_ref, chosen_ref, part_ref, high_ref, low_ref):
    adj = split(msg_ref[: msg_ref.shape[0] - INFO, :])
    sets = msg_ref.shape[1]
    chosen = chosen_ref[...]
    grid = pair_nn(split(basis(fact_ref[...])), adj)
    part = nn(chosen, jnp.concatenate(split(grid), axis=1))
    part_ref[...] = part[:, :sets] + part[:, sets:]
    high, low = split(basis(peer_ref[...]))
    high_ref[...] = nn(chosen, high).astype(bf16)
    low_ref[...] = nn(chosen, low).astype(bf16)


def third_kernel(msg_ref, own_ref, part_ref, high_ref, low_ref, *chunk_refs):
    chunk = part_ref.shape[0] // len(chunk_refs)
    scen = msg_ref.shape[0] - INFO
    adj = split(msg_ref[:scen, :])
    xva = msg_ref[scen:, :] + own_ref[scen:, :]
    for j, ref in enumerate(chunk_refs):
        rows = slice(j * chunk, (j + 1) * chunk)
        ref[:chunk, :] = part_ref[rows, :] + pair_nn((high_ref[rows, :], low_ref[rows, :]), adj)
        ref[chunk:, :] = xva


def feature_kernel(n_trade, *refs):
    blocks, folded_refs, (out_hbm, out_ref, sem) = refs[:n_trade], refs[n_trade : 2 * n_trade], refs[2 * n_trade :]
    (high, low), columns = blocks_of(blocks)
    total = jnp.zeros(out_ref.shape, f32)
    for k in range(n_trade):
        party, thr, wgt = info_of(blocks[k])
        same = same_as(columns, party)
        netted = nn(high, same) + nn(low, same)
        adj_high, adj_low = split(wgt * jax.nn.sigmoid(netted - thr))
        fold_high, fold_low = split(folded_refs[k][...])
        total = total + nt(fold_high, adj_high) + nt(fold_low, adj_high) + nt(fold_high, adj_low)
    out_ref[...] = total
    copy = pltpu.make_async_copy(out_ref, out_hbm, sem)
    copy.start()
    copy.wait()


def last_kernel(n_chunks, scale, member_ref, *refs):
    chunk_refs, (xva_hbm, out_hbm, xva_ref, out_ref, sems) = refs[:n_chunks], refs[n_chunks:]
    rows, cols = out_hbm.shape
    total = chunk_refs[0][...]
    for ref in chunk_refs[1:]:
        total = total + ref[...]
    total = total * scale
    xva_ref[...] = total[rows : rows + 1, :]
    first = pltpu.make_async_copy(xva_ref, xva_hbm, sems.at[0])
    first.start()
    high, low = split(total[:rows, :])
    copies = [first]
    pieces = sems.shape[0] - 1
    wide = cols // pieces
    for i in range(pieces):
        part = member_ref[:, i * wide : (i + 1) * wide]
        out_ref[:, i * wide : (i + 1) * wide] = nn(high, part) + nn(low, part)
        copies.append(
            pltpu.make_async_copy(
                out_ref.at[:, pl.ds(i * wide, wide)], out_hbm.at[:, pl.ds(i * wide, wide)], sems.at[i + 1]
            )
        )
        copies[-1].start()
    for copy in copies:
        copy.wait()


def call(kernel, out_shape, in_specs, args, scratch=(), flops=5 * 10**8, limit=None):
    args = [
        pltpu.with_memory_space_constraint(arg, pltpu.VMEM if spec is VMEM else pltpu.HBM)
        for arg, spec in zip(args, in_specs)
    ]
    specs = [HBM if isinstance(shape, jax.ShapeDtypeStruct) else VMEM for shape in out_shape]
    return pl.pallas_call(
        kernel,
        out_shape=out_shape,
        in_specs=in_specs,
        out_specs=specs,
        scratch_shapes=scratch,
        cost_estimate=pl.CostEstimate(flops=flops, bytes_accessed=10**5, transcendentals=0),
        compiler_params=pltpu.CompilerParams(vmem_limit_bytes=limit),
    )(*args)


def send(value, axis, k):
    return lax.ppermute(value, axis, [(i, i ^ k) for i in range(lax.axis_size(axis))])


def local(
    factors, feat_factor, feat_degree, coefficients, set_of_trade, party_of_set, threshold, weight
):
    n_trade, n_scen = lax.axis_size("trade"), lax.axis_size("scen")
    scen, nfac = factors.shape
    width, cols = coefficients.shape
    sets = cols // SET_SIZE
    lines = width // BLOCK
    own, chunk, grid = width // n_trade, width // n_scen, MAXDEG * nfac
    struct, vmem, dma = jax.ShapeDtypeStruct, pltpu.VMEM, pltpu.SemaphoreType.DMA
    i32 = jnp.int32
    outs = call(
        functools.partial(first_kernel, n_trade),
        [vmem((own, sets), f32)] * n_trade
        + [vmem((scen + INFO, sets), f32), vmem((nfac, scen), f32), vmem((lines, BLOCK), i32)]
        + [vmem((INFO, sets), f32), vmem((sets, cols), bf16)],
        [HBM] * 8,
        [
            factors.T,
            feat_factor.reshape(lines, BLOCK),
            feat_degree.reshape(lines, BLOCK),
            coefficients,
            set_of_trade.reshape(1, cols),
            party_of_set.reshape(1, sets),
            threshold.reshape(n_trade, sets),
            weight.reshape(n_trade, sets),
        ],
        [
            vmem((nfac, scen), f32),
            vmem((lines, BLOCK), i32),
            vmem((lines, BLOCK), i32),
            vmem((1, cols), i32),
            vmem((1, sets), i32),
            vmem((n_trade, sets), f32),
            vmem((n_trade, sets), f32),
            vmem((lines, BLOCK, cols), f32),
            dma((7,)),
            dma((lines,)),
        ],
        limit=32 << 20,
    )
    folded, (expo, fact, key, side, member) = outs[:n_trade], outs[n_trade:]
    blocks = [expo] + [None] * (n_trade - 1)
    for k in range(2, n_trade, 2):
        blocks[k] = send(expo, "trade", k)
    blocks[1] = send(expo, "trade", 1)
    for k in range(2, n_trade, 2):
        blocks[k + 1] = send(blocks[k], "trade", 1)
    peer_fact = send(fact, "scen", 1)
    (chosen,) = call(
        functools.partial(choose_kernel, n_scen),
        [vmem((width // 2, grid), bf16)],
        [VMEM],
        [key],
        [vmem((width, BLOCK), f32)],
        limit=8 << 20,
    )
    total = []
    for here in (blocks[:2], blocks[2::2]):
        total = call(
            functools.partial(net_kernel, len(here)),
            [vmem((scen, 2 * sets), f32)],
            [VMEM] * (len(here) + 1 + len(total)),
            [*here, expo, *total],
            limit=8 << 20,
        )
    here = blocks[3::2]
    (msg,) = call(
        functools.partial(second_kernel, len(here)),
        [vmem((scen + INFO, sets), f32)],
        [VMEM] * (len(here) + 4),
        [*here, expo, *total, side, peer_fact],
        [vmem((scen, 2 * sets), f32)],
        limit=8 << 20,
    )
    peer = send(msg, "scen", 1)
    middle = call(
        middle_kernel,
        [vmem((width // 2, sets), f32)] + [vmem((width // 2, scen), bf16)] * 2,
        [VMEM] * 4,
        [msg, fact, peer_fact, chosen],
        limit=8 << 20,
    )
    msg, *later = lax.optimization_barrier((msg, *folded[2:]))
    later = [folded[1], *later]
    moved = [folded[0]] + [send(later[k - 1], "trade", k) for k in range(1, n_trade)]
    chunks = call(
        third_kernel, [vmem((chunk + INFO, sets), f32)] * (n_scen // 2), [VMEM] * 5, [peer, msg, *middle], limit=8 << 20
    )
    chunks = [chunks[0]] + [
        send(chunks[j], "scen", 2 * j)
        for j in [*range(n_scen // 2 - 1, n_scen // 4, -1), *range(1, n_scen // 4), *range(n_scen // 4, n_scen // 4 + 1)]
    ]
    (feature_sens,) = call(
        functools.partial(feature_kernel, n_trade),
        [struct((own, scen), f32)],
        [VMEM] * (2 * n_trade),
        [*blocks, *moved],
        [vmem((own, scen), f32), dma],
        flops=2 * 10**9,
        limit=8 << 20,
    )
    xva, coef_sens = call(
        functools.partial(last_kernel, n_scen // 2, 1.0 / (scen * n_scen)),
        [struct((1, sets), f32), struct((chunk, cols), f32)],
        [VMEM] * (n_scen // 2 + 1),
        [member, *chunks],
        [vmem((1, sets), f32), vmem((chunk, cols), f32), dma((5,))],
        limit=8 << 20,
    )
    return (xva.reshape(sets), coef_sens, feature_sens)


def solution(mesh):
    in_specs = (P("scen", None), P(), P(), P(None, "trade"), P("trade"), P("trade"), P(), P())
    out_specs = (P("trade"), P("scen", "trade"), P("trade", "scen"))
    return jax.shard_map(local, mesh=mesh, in_specs=in_specs, out_specs=out_specs, check_vma=False)
```

```python
import functools

import jax
import jax.numpy as jnp
from jax import lax
from jax.experimental import pallas as pl
from jax.experimental.pallas import tpu as pltpu
from jax.sharding import PartitionSpec as P


MAXDEG = 12
SET_SIZE = 16
INFO = 8
BLOCK = 128

f32 = jnp.float32
bf16 = jnp.bfloat16
VMEM = pl.BlockSpec(memory_space=pltpu.VMEM)
HBM = pl.BlockSpec(memory_space=pltpu.HBM)


def split(value):
    high = value.astype(bf16)
    low = (value - high.astype(f32)).astype(bf16)
    return high, low


def nn(left, right):
    return lax.dot_general(left, right, (((1,), (0,)), ((), ())), preferred_element_type=f32)


def nt(left, right):
    return lax.dot_general(left, right, (((1,), (1,)), ((), ())), preferred_element_type=f32)


def pair_nn(left, right):
    cols = right[0].shape[1]
    both = nn(left[0], jnp.concatenate(right, axis=1))
    return both[:, :cols] + both[:, cols:] + nn(left[1], right[0])


def iota(shape, dim):
    return lax.broadcasted_iota(jnp.int32, shape, dim)


def column(row):
    n = row.shape[1]
    return jnp.transpose(jnp.broadcast_to(row.astype(f32), (n, n)))


def one_hot(test):
    return jnp.where(test, f32(1), f32(0)).astype(bf16)


def pick(table, ids):
    rows, lanes = table.shape
    total = jnp.zeros((1, ids.shape[1]), f32)
    for r in range(rows):
        here = column(table[r : r + 1, :])
        where = iota((lanes, ids.shape[1]), 0) + r * lanes == ids
        total = total + jnp.sum(jnp.where(where, here[:, : ids.shape[1]], 0.0), axis=0, keepdims=True)
    return total


def basis(points):
    before, current = jnp.ones_like(points), points
    rows = [current]
    for _ in range(2, MAXDEG + 1):
        before, current = current, 2.0 * points * current - before
        rows.append(current)
    return jnp.concatenate(rows, axis=0)


def first_kernel(n_trade, *refs):
    ins, rest = refs[:8], refs[8:]
    folded_refs, rest = rest[:n_trade], rest[n_trade:]
    expo_ref, fact_out, key_out, side_out, member_out = rest[:5]
    fact_ref, factor_ref, degree_ref, set_ref, party_ref, thr_ref, wgt_ref, coef_buf, small, sems = rest[5:]
    fact_hbm, factor_hbm, degree_hbm, coef_hbm, set_hbm, party_hbm, thr_hbm, wgt_hbm = ins
    me = lax.axis_index("trade")
    width, cols = coef_hbm.shape
    sets = cols // SET_SIZE
    nfac, scen = fact_ref.shape
    own = width // n_trade
    steps = width // BLOCK
    per = own // BLOCK

    loads = [
        pltpu.make_async_copy(source, target, small.at[i])
        for i, (source, target) in enumerate(
            [
                (fact_hbm, fact_ref),
                (set_hbm, set_ref),
                (factor_hbm, factor_ref),
                (degree_hbm, degree_ref),
                (party_hbm, party_ref),
                (thr_hbm, thr_ref),
                (wgt_hbm, wgt_ref),
            ]
        )
    ]

    def start_row(step):
        return pl.multiple_of((me ^ (step // per)) * own + (step % per) * BLOCK, BLOCK)

    def copy(step):
        return pltpu.make_async_copy(
            coef_hbm.at[pl.ds(start_row(step), BLOCK), :], coef_buf.at[step], sems.at[step]
        )

    for load in loads:
        load.start()
    for step in range(steps):
        copy(step).start(priority=1)
    for load in loads:
        load.wait()
    member = jnp.where(set_ref[...] - me * sets == iota((sets, cols), 0), f32(1), f32(0))
    member_out[...] = member.astype(bf16)
    turned_member = jnp.transpose(member).astype(bf16)
    twice = jnp.concatenate([turned_member, turned_member], axis=0)
    fact_out[...] = fact_ref[...]
    table = split(jnp.transpose(basis(fact_ref[...])))
    key_out[...] = factor_ref[...] + nfac * (degree_ref[...] - 1)
    party = party_ref[...]
    thr_row = pick(thr_ref[...], party)
    wgt_row = pick(wgt_ref[...], party)
    line = iota((INFO, sets), 0)
    expo_ref[scen:, :] = jnp.where(line == 0, party.astype(f32), jnp.where(line == 1, thr_row, wgt_row))
    side_out[...] = jnp.where(line == 0, thr_ref[pl.ds(me, 1), :], wgt_ref[pl.ds(me, 1), :])
    keys = [key_out[pl.ds(lax.div(start_row(step), BLOCK), 1), :] for step in range(steps)]
    chosen = one_hot(iota((MAXDEG * nfac, width), 0) == jnp.concatenate(keys, axis=1))
    phi = [nn(part, chosen).astype(bf16) for part in table]
    done, total = 0, None
    for size in (steps // 2, steps - steps // 2):
        group = range(done, done + size)
        for step in group:
            copy(step).wait()
        highs, lows = [], []
        for step in group:
            coef_high, coef_low = split(coef_buf[step])
            folded = nn(jnp.concatenate([coef_high, coef_low], axis=1), twice)
            folded_refs[step // per][pl.ds((step % per) * BLOCK, BLOCK), :] = folded
            high, low = split(folded)
            highs.append(high)
            lows.append(low)
        here = slice(done * BLOCK, (done + size) * BLOCK)
        part = pair_nn(
            [piece[:, here] for piece in phi],
            [jnp.concatenate(highs, axis=0), jnp.concatenate(lows, axis=0)],
        )
        total = part if total is None else total + part
        done += size
    expo_ref[:scen, :] = total


def blocks_of(refs):
    scen = refs[0].shape[0] - INFO
    expo = [split(ref[:scen, :]) for ref in refs]
    pieces = [jnp.concatenate([e[i] for e in expo], axis=1) for i in range(2)]
    return pieces, [column(ref[scen : scen + 1, :]) for ref in refs]


def same_as(columns, row):
    return one_hot(jnp.concatenate([here == row for here in columns], axis=0))


def info_of(ref):
    info = ref[ref.shape[0] - INFO :, :]
    return info[0:1, :], info[1:2, :], info[2:3, :]


def net_kernel(n_blocks, *refs):
    blocks, own_ref, *total, out_ref = refs[:n_blocks], *refs[n_blocks:]
    trade = lax.axis_index("trade")
    sets = own_ref.shape[1]
    (high, low), columns = blocks_of(blocks)
    party, _, _ = info_of(own_ref)
    mine = (iota((1, sets), 1) + trade * sets).astype(f32)
    right = jnp.concatenate([same_as(columns, party), same_as(columns, mine)], axis=1)
    netted = nn(high, right) + nn(low, right)
    out_ref[...] = total[0][...] + netted if total else netted


def second_kernel(n_blocks, *refs):
    *ins, side_ref, _, msg_ref, net_ref = refs
    net_kernel(n_blocks, *ins, net_ref)
    own_ref = ins[n_blocks]
    scen, sets = own_ref.shape[0] - INFO, own_ref.shape[1]
    _, thr, wgt = info_of(own_ref)
    msg_ref[:scen, :] = wgt * jax.nn.sigmoid(net_ref[:, :sets] - thr)
    soft = jax.nn.softplus(net_ref[:, sets:] - side_ref[0:1, :])
    msg_ref[scen:, :] = jnp.broadcast_to(
        jnp.sum(soft, axis=0, keepdims=True) * side_ref[1:2, :], (INFO, sets)
    )


def choose_kernel(n_scen, key_ref, chosen_ref, column_ref):
    me = lax.axis_index("scen")
    lines = key_ref.shape[0]
    chunk = lines * BLOCK // n_scen
    for i in range(lines):
        column_ref[i * BLOCK : (i + 1) * BLOCK, :] = column(key_ref[i : i + 1, :])
    for j in range(n_scen // 2):
        here = column_ref[pl.ds(pl.multiple_of((me ^ (2 * j)) * chunk, chunk), chunk), :].astype(jnp.int32)
        for i in range(chosen_ref.shape[1] // BLOCK):
            chosen_ref[j * chunk : (j + 1) * chunk, i * BLOCK : (i + 1) * BLOCK] = one_hot(
                here == iota(here.shape, 1) + i * BLOCK
            )


def middle_kernel(msg_ref, fact_ref, peer_ref, chosen_ref, part_ref, high_ref, low_ref):
    adj = split(msg_ref[: msg_ref.shape[0] - INFO, :])
    sets = msg_ref.shape[1]
    chosen = chosen_ref[...]
    grid = pair_nn(split(basis(fact_ref[...])), adj)
    part = nn(chosen, jnp.concatenate(split(grid), axis=1))
    part_ref[...] = part[:, :sets] + part[:, sets:]
    high, low = split(basis(peer_ref[...]))
    high_ref[...] = nn(chosen, high).astype(bf16)
    low_ref[...] = nn(chosen, low).astype(bf16)


def third_kernel(msg_ref, own_ref, part_ref, high_ref, low_ref, *chunk_refs):
    chunk = part_ref.shape[0] // len(chunk_refs)
    scen = msg_ref.shape[0] - INFO
    adj = split(msg_ref[:scen, :])
    xva = msg_ref[scen:, :] + own_ref[scen:, :]
    for j, ref in enumerate(chunk_refs):
        rows = slice(j * chunk, (j + 1) * chunk)
        ref[:chunk, :] = part_ref[rows, :] + pair_nn((high_ref[rows, :], low_ref[rows, :]), adj)
        ref[chunk:, :] = xva


def feature_kernel(n_trade, *refs):
    blocks, folded_refs, (out_hbm, out_ref, sem) = refs[:n_trade], refs[n_trade : 2 * n_trade], refs[2 * n_trade :]
    (high, low), columns = blocks_of(blocks)
    total = jnp.zeros(out_ref.shape, f32)
    for k in range(n_trade):
        party, thr, wgt = info_of(blocks[k])
        same = same_as(columns, party)
        netted = nn(high, same) + nn(low, same)
        adj_high, adj_low = split(wgt * jax.nn.sigmoid(netted - thr))
        fold_high, fold_low = split(folded_refs[k][...])
        total = total + nt(fold_high, adj_high) + nt(fold_low, adj_high) + nt(fold_high, adj_low)
    out_ref[...] = total
    copy = pltpu.make_async_copy(out_ref, out_hbm, sem)
    copy.start()
    copy.wait()


def last_kernel(n_chunks, scale, member_ref, *refs):
    chunk_refs, (xva_hbm, out_hbm, xva_ref, out_ref, sems) = refs[:n_chunks], refs[n_chunks:]
    rows, cols = out_hbm.shape
    total = chunk_refs[0][...]
    for ref in chunk_refs[1:]:
        total = total + ref[...]
    total = total * scale
    xva_ref[...] = total[rows : rows + 1, :]
    first = pltpu.make_async_copy(xva_ref, xva_hbm, sems.at[0])
    first.start()
    high, low = split(total[:rows, :])
    copies = [first]
    pieces = sems.shape[0] - 1
    wide = cols // pieces
    for i in range(pieces):
        part = member_ref[:, i * wide : (i + 1) * wide]
        out_ref[:, i * wide : (i + 1) * wide] = nn(high, part) + nn(low, part)
        copies.append(
            pltpu.make_async_copy(
                out_ref.at[:, pl.ds(i * wide, wide)], out_hbm.at[:, pl.ds(i * wide, wide)], sems.at[i + 1]
            )
        )
        copies[-1].start()
    for copy in copies:
        copy.wait()


def call(kernel, out_shape, in_specs, args, scratch=(), flops=5 * 10**8, limit=None):
    args = [
        pltpu.with_memory_space_constraint(arg, pltpu.VMEM if spec is VMEM else pltpu.HBM)
        for arg, spec in zip(args, in_specs)
    ]
    specs = [HBM if isinstance(shape, jax.ShapeDtypeStruct) else VMEM for shape in out_shape]
    return pl.pallas_call(
        kernel,
        out_shape=out_shape,
        in_specs=in_specs,
        out_specs=specs,
        scratch_shapes=scratch,
        cost_estimate=pl.CostEstimate(flops=flops, bytes_accessed=10**5, transcendentals=0),
        compiler_params=pltpu.CompilerParams(vmem_limit_bytes=limit),
    )(*args)


def send(value, axis, k):
    return lax.ppermute(value, axis, [(i, i ^ k) for i in range(lax.axis_size(axis))])


def local(
    factors, feat_factor, feat_degree, coefficients, set_of_trade, party_of_set, threshold, weight
):
    n_trade, n_scen = lax.axis_size("trade"), lax.axis_size("scen")
    scen, nfac = factors.shape
    width, cols = coefficients.shape
    sets = cols // SET_SIZE
    lines = width // BLOCK
    own, chunk, grid = width // n_trade, width // n_scen, MAXDEG * nfac
    struct, vmem, dma = jax.ShapeDtypeStruct, pltpu.VMEM, pltpu.SemaphoreType.DMA
    i32 = jnp.int32
    outs = call(
        functools.partial(first_kernel, n_trade),
        [vmem((own, sets), f32)] * n_trade
        + [vmem((scen + INFO, sets), f32), vmem((nfac, scen), f32), vmem((lines, BLOCK), i32)]
        + [vmem((INFO, sets), f32), vmem((sets, cols), bf16)],
        [HBM] * 8,
        [
            factors.T,
            feat_factor.reshape(lines, BLOCK),
            feat_degree.reshape(lines, BLOCK),
            coefficients,
            set_of_trade.reshape(1, cols),
            party_of_set.reshape(1, sets),
            threshold.reshape(n_trade, sets),
            weight.reshape(n_trade, sets),
        ],
        [
            vmem((nfac, scen), f32),
            vmem((lines, BLOCK), i32),
            vmem((lines, BLOCK), i32),
            vmem((1, cols), i32),
            vmem((1, sets), i32),
            vmem((n_trade, sets), f32),
            vmem((n_trade, sets), f32),
            vmem((lines, BLOCK, cols), f32),
            dma((7,)),
            dma((lines,)),
        ],
        limit=32 << 20,
    )
    folded, (expo, fact, key, side, member) = outs[:n_trade], outs[n_trade:]
    blocks = [expo] + [None] * (n_trade - 1)
    for k in range(2, n_trade, 2):
        blocks[k] = send(expo, "trade", k)
    blocks[1] = send(expo, "trade", 1)
    for k in range(2, n_trade, 2):
        blocks[k + 1] = send(blocks[k], "trade", 1)
    peer_fact = send(fact, "scen", 1)
    (chosen,) = call(
        functools.partial(choose_kernel, n_scen),
        [vmem((width // 2, grid), bf16)],
        [VMEM],
        [key],
        [vmem((width, BLOCK), f32)],
        limit=8 << 20,
    )
    total = []
    for here in (blocks[:2], blocks[2::2]):
        total = call(
            functools.partial(net_kernel, len(here)),
            [vmem((scen, 2 * sets), f32)],
            [VMEM] * (len(here) + 1 + len(total)),
            [*here, expo, *total],
            limit=8 << 20,
        )
    here = blocks[3::2]
    (msg,) = call(
        functools.partial(second_kernel, len(here)),
        [vmem((scen + INFO, sets), f32)],
        [VMEM] * (len(here) + 4),
        [*here, expo, *total, side, peer_fact],
        [vmem((scen, 2 * sets), f32)],
        limit=8 << 20,
    )
    peer = send(msg, "scen", 1)
    middle = call(
        middle_kernel,
        [vmem((width // 2, sets), f32)] + [vmem((width // 2, scen), bf16)] * 2,
        [VMEM] * 4,
        [msg, fact, peer_fact, chosen],
        limit=8 << 20,
    )
    msg, *later = lax.optimization_barrier((msg, *folded[1:]))
    moved = [folded[0]] + [send(later[k - 1], "trade", k) for k in range(1, n_trade)]
    chunks = call(
        third_kernel, [vmem((chunk + INFO, sets), f32)] * (n_scen // 2), [VMEM] * 5, [peer, msg, *middle], limit=8 << 20
    )
    chunks = [chunks[0]] + [
        send(chunks[j], "scen", 2 * j)
        for j in [*range(n_scen // 4, n_scen // 2), *range(1, n_scen // 4)]
    ]
    (feature_sens,) = call(
        functools.partial(feature_kernel, n_trade),
        [struct((own, scen), f32)],
        [VMEM] * (2 * n_trade),
        [*blocks, *moved],
        [vmem((own, scen), f32), dma],
        flops=2 * 10**9,
        limit=8 << 20,
    )
    xva, coef_sens = call(
        functools.partial(last_kernel, n_scen // 2, 1.0 / (scen * n_scen)),
        [struct((1, sets), f32), struct((chunk, cols), f32)],
        [VMEM] * (n_scen // 2 + 1),
        [member, *chunks],
        [vmem((1, sets), f32), vmem((chunk, cols), f32), dma((5,))],
        limit=8 << 20,
    )
    return (xva.reshape(sets), coef_sens, feature_sens)


def solution(mesh):
    in_specs = (P("scen", None), P(), P(), P(None, "trade"), P("trade"), P("trade"), P(), P())
    out_specs = (P("trade"), P("scen", "trade"), P("trade", "scen"))
    return jax.shard_map(local, mesh=mesh, in_specs=in_specs, out_specs=out_specs, check_vma=False)
```
